256 devices in a mesh: grp: 8 (over z), exp: 16 (over x, y), rep: 2 (over core).
Axes of the slice: x: 4, y: 4, z: 8, core: 2. Of those that a mesh axis runs over, the one named last changes fastest.
Arguments:
- tokens: bfloat16 [8192, 2048], P(('grp', 'exp', 'rep')), may hold values from -6 to 6
- cotangent: bfloat16 [8192, 2048], P(('grp', 'exp', 'rep')), may hold values from -6 to 6
- expert_ids: int32 [8192, 8], P(('grp', 'exp', 'rep')), may hold values from 0 to 127, all different within a row; in each aligned block of 32 rows (0 to 31, 32 to 63, ...) at most 3 rows name the same one
- gate_probs: float32 [8192, 8], P(('grp', 'exp', 'rep')), may hold values from 0.05 to 0.6
- gate_weight: bfloat16 [128, 2048, 768], P(('grp', 'exp'), 'rep'), may hold values from -0.125 to 0.125
- up_weight: bfloat16 [128, 2048, 768], P(('grp', 'exp'), 'rep'), may hold values from -0.125 to 0.125
- down_weight: bfloat16 [128, 768, 2048], P(('grp', 'exp'), 'rep'), may hold values from -0.21875 to 0.21875
Outputs:
- layer_out: bfloat16 [8192, 2048], P(('grp', 'exp', 'rep'))
- token_grad: bfloat16 [8192, 2048], P(('grp', 'exp', 'rep'))
- gate_grad: bfloat16 [128, 2048, 768], P(('grp', 'exp'), 'rep')
- up_grad: bfloat16 [128, 2048, 768], P(('grp', 'exp'), 'rep')
- down_grad: bfloat16 [128, 768, 2048], P(('grp', 'exp'), 'rep')
The draws below stay inside these ranges and needn't reach their ends.
Inputs may be any that keep to these rules, and one draw needn't show every extreme that they name: `expert_ids`: each token names 8 different experts. Among the 32 tokens of one device, no expert is named more than 3 times, and in some device one expert is named exactly 3 times.
All inputs are finite; a program needn't handle non-finite values.
Results may differ from the reference program's by a relative error of at most 0.0065.
Values may be sent and summed in bfloat16 or wider, within the bound.
A program may use at most 128 MiB of HBM per device.

```python
import math
import jax
import jax.numpy as jnp
import numpy as np
from jax import lax

D = 2048
FF = 768
TOP = 8
TOK_DEV = 32
EXPERTS = 128
TOKENS = 8192
CAP = 3
N_REP = 2


def shard_levels(key, extent, pieces, low, top_value):
    def one(dim, blocks):
        draws = jax.random.uniform(jax.random.fold_in(jax.random.fold_in(key, 6), dim), (blocks,), jnp.float32, low / len(pieces), top_value / len(pieces))
        return jnp.repeat(jnp.exp(draws), extent[dim] // blocks).reshape((-1,) + (1,) * (len(extent) - dim - 1))

    level = one(*pieces[0])
    for cut in pieces[1:]:
        level = level * one(*cut)
    return level


def assign_block(rng, own, number, rows, count, top, bound, skew):
    sequence = jax.random.permutation(rng, count)
    crowded, ordinary = shares(count, rows * top, bound, skew, True), shares(count, rows * top, bound, skew, False)
    places = jnp.arange(count)

    def named(lengths, offset_by):
        used = int((lengths > 0).sum())
        fixed = max(1, used // 4)
        shifted = fixed + (places - fixed + offset_by * (used - fixed)) % max(1, count - fixed)
        return jnp.zeros((count,), jnp.int32).at[sequence[jnp.where(places < fixed, places, shifted)]].set(jnp.asarray(lengths, jnp.int32))

    lengths = jnp.where(number % 4 == 0, named(crowded, number // 4), named(ordinary, number - number // 4 - 1))
    mixed = jax.random.permutation(jax.random.fold_in(own, 3), count)
    donor, sink = mixed[0:count // 2 * 2:2], mixed[1:count // 2 * 2:2]
    room = jnp.minimum(lengths[donor] - 1, bound - lengths[sink]) // 2
    room = jnp.where((donor == sequence[0]) | (sink == sequence[0]) | (lengths[sink] == 0), 0, jnp.maximum(room, 0))
    shifted = jax.random.randint(jax.random.fold_in(own, 4), (count // 2,), 0, 1 << 20) % (room + 1)
    lengths = lengths.at[donor].add(-shifted).at[sink].add(shifted)
    labels = jnp.searchsorted(jnp.cumsum(lengths), jnp.arange(rows * top), side="right").astype(jnp.int32)
    listing = labels.reshape(top, rows).T
    listing = listing[jax.random.permutation(jax.random.fold_in(own, 1), rows)]
    offset_by = jax.random.randint(jax.random.fold_in(own, 2), (rows, 1), 0, top)
    return jnp.take_along_axis(listing, (jnp.arange(top)[None, :] + offset_by) % top, axis=1)


def shares(number_of, total, reach, slope, full):
    portions = [(1 << 20) // math.isqrt(rank ** slope) + 1 for rank in range(1, number_of + 1)]
    largest = reach if full else min(reach, max(-(-total // number_of), total * portions[0] // sum(portions)))
    least = 1 if total - largest >= number_of - 1 else 0
    counts, rest = [largest] + [least] * (number_of - 1), total - largest - least * (number_of - 1)
    while rest > 0:
        free = [i for i in range(1, number_of) if counts[i] < largest] or [i for i in range(1, number_of) if counts[i] < reach]
        mass, left = sum([portions[i] for i in free]), rest
        for i in free:
            more = min(reach - counts[i], max(1, left * portions[i] // mass), rest)
            counts[i] = counts[i] + more
            rest = rest - more
    return np.array(counts)


def normal_values(rng, dims, deviation, limit, shards=(), held_as=jnp.bfloat16):
    gain = shard_levels(rng, dims, shards, -0.22, 0.18) if shards else 1.0
    result = jax.random.normal(rng, dims, jnp.float32) * deviation * gain
    return jnp.minimum(jnp.maximum(result, -limit), limit).astype(held_as)


def setup_inputs(seed: int = 0) -> dict:
    key_list = jax.random.split(jax.random.key(seed), 8)
    tokens = normal_values(key_list[0], (TOKENS, D), 1.0, 6.0, ((0, 256),))
    cotangent = normal_values(key_list[1], (TOKENS, D), 1.0, 6.0, ((0, 256),))
    expert_ids_keys = jax.random.split(jax.random.fold_in(key_list[2], 1), TOKENS // TOK_DEV)
    expert_ids_turns = jax.random.permutation(jax.random.fold_in(key_list[2], 3), TOKENS // TOK_DEV)
    expert_ids = jax.vmap(lambda own, number: assign_block(jax.random.fold_in(key_list[2], 2), own, number, TOK_DEV, EXPERTS, TOP, CAP, 2))(expert_ids_keys, expert_ids_turns).reshape((TOKENS, TOP))
    gate_probs = jnp.clip(jnp.exp(math.log(0.6) - 2.4849067 * jax.random.uniform(key_list[3], (TOKENS, TOP), jnp.float32) ** shard_levels(key_list[3], (TOKENS, TOP), ((0, 256),), -0.2, 0.2)), 0.05, 0.6)
    gate_weight = normal_values(key_list[4], (EXPERTS, D, FF), D ** -0.5, 0.125, ((0, 128), (1, 2)))
    up_weight = normal_values(key_list[5], (EXPERTS, D, FF), D ** -0.5, 0.125, ((0, 128), (1, 2)))
    down_weight = normal_values(key_list[6], (EXPERTS, FF, D), FF ** -0.5, 0.21875, ((0, 128), (1, 2)))
    return {"tokens": tokens, "cotangent": cotangent, "expert_ids": expert_ids, "gate_probs": gate_probs, "gate_weight": gate_weight, "up_weight": up_weight, "down_weight": down_weight}


def expert_pass(rows_in, rows_scaled, gate_mat, up_mat, down_mat):
    gate_pre = jnp.dot(rows_in, gate_mat, preferred_element_type=jnp.float32)
    up_pre = jnp.dot(rows_in, up_mat, preferred_element_type=jnp.float32)
    sigma = jax.nn.sigmoid(gate_pre)
    act = gate_pre * sigma
    hidden = (act * up_pre).astype(jnp.bfloat16)
    out_rows = jnp.dot(hidden, down_mat, preferred_element_type=jnp.float32).astype(jnp.bfloat16)
    dhidden = jnp.dot(rows_scaled, down_mat.T, preferred_element_type=jnp.float32)
    dgate = (dhidden * up_pre * sigma * (1.0 + gate_pre * (1.0 - sigma))).astype(jnp.bfloat16)
    dup = (dhidden * act).astype(jnp.bfloat16)
    grad_rows = (jnp.dot(dgate, gate_mat.T, preferred_element_type=jnp.float32)
                 + jnp.dot(dup, up_mat.T, preferred_element_type=jnp.float32)).astype(jnp.bfloat16)
    grad_gate = jnp.dot(rows_in.T, dgate, preferred_element_type=jnp.float32)
    grad_up = jnp.dot(rows_in.T, dup, preferred_element_type=jnp.float32)
    grad_down = jnp.dot(hidden.T, rows_scaled, preferred_element_type=jnp.float32)
    return out_rows, grad_rows, grad_gate, grad_up, grad_down


def reference(tokens, cotangent, expert_ids, gate_probs, gate_weight, up_weight, down_weight):
    row_count = TOKENS * TOP
    slot_count = EXPERTS * CAP
    flat_ids = expert_ids.reshape(row_count)
    flat_probs = gate_probs.reshape(row_count)
    row_token = jnp.arange(row_count, dtype=jnp.int32) // TOP
    row_replica = (row_token // TOK_DEV) % N_REP

    def per_expert(carry, expert):
        out_sum, grad_sum = carry
        totals = [jnp.zeros((D, FF), jnp.float32), jnp.zeros((D, FF), jnp.float32), jnp.zeros((FF, D), jnp.float32)]
        for replica in range(N_REP):
            chosen = (flat_ids == expert) & (row_replica == replica)
            index = jnp.nonzero(chosen, size=slot_count, fill_value=row_count)[0].astype(jnp.int32)
            token_index = (index // TOP).astype(jnp.int32)
            rows_in = jnp.take(tokens, token_index, axis=0, mode="fill", fill_value=0)
            rows_dy = jnp.take(cotangent, token_index, axis=0, mode="fill", fill_value=0)
            probs = jnp.take(flat_probs, index, mode="fill", fill_value=0)
            rows_scaled = (probs[:, None] * rows_dy.astype(jnp.float32)).astype(jnp.bfloat16)
            out_rows, grad_rows, grad_gate, grad_up, grad_down = expert_pass(
                rows_in, rows_scaled, gate_weight[expert], up_weight[expert], down_weight[expert])
            out_sum = out_sum.at[token_index].add(probs[:, None] * out_rows.astype(jnp.float32), mode="drop")
            grad_sum = grad_sum.at[token_index].add(grad_rows.astype(jnp.float32), mode="drop")
            partials = [grad_gate, grad_up, grad_down]
            for slot in range(3):
                rounded = lax.optimization_barrier(partials[slot].astype(jnp.bfloat16))
                totals[slot] = totals[slot] + rounded.astype(jnp.float32)
        return (out_sum, grad_sum), tuple(item.astype(jnp.bfloat16) for item in totals)

    start = (jnp.zeros((TOKENS, D), jnp.float32), jnp.zeros((TOKENS, D), jnp.float32))
    (out_sum, grad_sum), grads = lax.scan(per_expert, start, jnp.arange(EXPERTS, dtype=jnp.int32))
    return out_sum.astype(jnp.bfloat16), grad_sum.astype(jnp.bfloat16), grads[0], grads[1], grads[2]
```

```python
import functools

import jax
import jax.numpy as jnp
from jax import lax
from jax.experimental import pallas as pl
from jax.experimental.pallas import tpu as pltpu
from jax.sharding import PartitionSpec as P

MESH = pl.DeviceIdType.MESH
F32 = jnp.float32
BF16 = jnp.bfloat16
RANKS = 3
HALF = 4
PIECES = 2 * HALF


def dot(a, b, dims):
    return lax.dot_general(a, b, (dims, ((), ())), preferred_element_type=F32)


NN = ((1,), (0,))
NT = ((1,), (1,))
TN = ((0,), (0,))


def kernel(
    zn, en,
    tok, cot, meta, wg, wu, wd,
    out_y, out_dx, out_g, out_u, out_d,
    ag, meta_v, wg_v, wu_v, wd_v, rank_v, prob_v, pick_f, prob_f, pick_b, pick_t, hi_t, lo_t,
    send, recv, gate, up, dh, hid, dgu, back, ret, part, rs_s, rs_r, own_gu, own_d, snd_gu, snd_d,
    rcv_gu, rcv_d, y_v, dx_v,
    l_sem, lm_sem, lw_sem, m_ssem, m_rsem, w_ssem, w_rsem, ag_ssem, ag_rsem, d_ssem, d_rsem, own_sem,
    b_ssem, b_rsem, bown_sem, rs_ssem, rs_rsem, g_ssem, g_rsem, o_sem,
):
    z = lax.axis_index("grp")
    c = lax.axis_index("exp")
    r = lax.axis_index("rep")
    o = 1 - r
    tn = ag.shape[2]
    w = ag.shape[3]
    rows = RANKS * zn
    slots = en * rows
    ff = gate.shape[1]
    fh = ff // 2
    lanes = 128
    per = lanes // tn
    long = zn // 2

    def hops(p, way):
        return long if (p % 2) == way else zn - 1 - long

    def step(way):
        return 1 if way == 0 else -1

    def there(way):
        return {"grp": lax.rem(z + step(way) + zn, zn)}

    def local(p):
        src = tok if p < HALF else cot
        return pltpu.make_async_copy(
            src.at[:, pl.ds((p % HALF) * w, w)], ag.at[p, z], l_sem.at[p])

    meta_in = pltpu.make_async_copy(meta, meta_v.at[z], lm_sem)
    meta_in.start()
    for p in range(PIECES):
        local(p).start()
    wq = HALF // 2
    half_gate = pl.ds(r * wq, wq)
    half_down = pl.ds(pl.multiple_of(r * fh, fh), fh)
    w_local = [
        pltpu.make_async_copy(wg, wg_v.at[half_gate], lw_sem.at[0]),
        pltpu.make_async_copy(wu, wu_v.at[half_gate], lw_sem.at[1]),
    ]
    for q in range(HALF):
        w_local.append(pltpu.make_async_copy(
            wd.at[:, pl.ds(q * w, w)], wd_v.at[q, half_down], lw_sem.at[2 + q]))
    for copy in w_local:
        copy.start()

    barrier = pltpu.get_barrier_semaphore()
    pl.semaphore_signal(barrier, inc=1, device_id={"rep": o}, device_id_type=MESH)

    def greet_grp(d, carry):
        pl.semaphore_signal(barrier, inc=1, device_id={"grp": lax.rem(z + d, zn)}, device_id_type=MESH)
        return carry

    def greet_exp(d, carry):
        pl.semaphore_signal(barrier, inc=1, device_id={"exp": lax.rem(c + d, en)}, device_id_type=MESH)
        return carry

    lax.fori_loop(1, zn, greet_grp, 0)
    lax.fori_loop(1, en, greet_exp, 0)
    pl.semaphore_wait(barrier, 1 + (zn - 1) + (en - 1))

    meta_in.wait()

    def send_meta(d, carry):
        pltpu.make_async_remote_copy(
            src_ref=meta_v.at[z], dst_ref=meta_v.at[z], send_sem=m_ssem, recv_sem=m_rsem,
            device_id={"grp": lax.rem(z + d, zn)}, device_id_type=MESH).start()
        return carry

    lax.fori_loop(1, zn, send_meta, 0)

    def ring(p, way, s):
        block = lax.rem(z - step(way) * s + zn, zn)
        return pltpu.make_async_remote_copy(
            src_ref=ag.at[p, block], dst_ref=ag.at[p, block],
            send_sem=ag_ssem.at[way, p, s], recv_sem=ag_rsem.at[way, p, s],
            device_id=there(way), device_id_type=MESH)

    def ring_recv(p, way, s):
        pltpu.make_async_copy(ag.at[p, 0], ag.at[p, 0], ag_rsem.at[way, p, s]).wait()

    def ring_step(p, s):
        if s == 0:
            local(p).wait()
        for way in (0, 1):
            if s < hops(p, way):
                if s > 0:
                    ring_recv(p, way, s - 1)
                ring(p, way, s).start()

    def weights_out():
        copies = [
            pltpu.make_async_remote_copy(
                src_ref=wg, dst_ref=wg_v.at[half_gate], send_sem=w_ssem.at[0], recv_sem=w_rsem.at[0],
                device_id={"rep": o}, device_id_type=MESH),
            pltpu.make_async_remote_copy(
                src_ref=wu, dst_ref=wu_v.at[half_gate], send_sem=w_ssem.at[1], recv_sem=w_rsem.at[1],
                device_id={"rep": o}, device_id_type=MESH),
        ]
        for q in range(HALF):
            copies.append(pltpu.make_async_remote_copy(
                src_ref=wd.at[:, pl.ds(q * w, w)], dst_ref=wd_v.at[q, half_down],
                send_sem=w_ssem.at[2 + q], recv_sem=w_rsem.at[2 + q],
                device_id={"rep": o}, device_id_type=MESH))
        return copies

    def tables():
        pltpu.make_async_copy(
            meta_v.at[pl.ds(0, zn - 1)], meta_v.at[pl.ds(0, zn - 1)], m_rsem).wait()
        row = lax.broadcasted_iota(jnp.int32, (lanes, lanes), 0)
        col = lax.broadcasted_iota(jnp.int32, (lanes, lanes), 1)
        before = ((row < col) & (row // tn == col // tn)).astype(F32).astype(BF16)
        mine = (lax.broadcasted_iota(jnp.int32, (en, lanes), 0) + en * z).astype(F32)
        sub = lax.broadcasted_iota(jnp.int32, (rows, lanes), 0)
        lane = lax.broadcasted_iota(jnp.int32, (rows, lanes), 1)
        want = (sub // zn).astype(F32)
        for h in range(zn // per):
            both = meta_v[h * per]
            for b in range(1, per):
                both = both + meta_v[h * per + b]
            named = jnp.zeros((en, lanes), F32)
            prob = jnp.zeros((en, lanes), F32)
            for k in range(8):
                hit = both[k:k + 1, :] == mine
                named = named + jnp.where(hit, 1.0, 0.0)
                prob = prob + jnp.where(hit, both[8 + k:9 + k, :], 0.0)
            rank = dot(named.astype(BF16), before, NN)
            rank_v[h] = jnp.where(named > 0.0, rank, -1.0)
            prob_v[h] = prob
            here = (sub % zn) == (h * per + lane // tn)
            for e in range(en):
                hit = (rank_v[h, e:e + 1, :] == want) & here
                at = (slice(e * rows, (e + 1) * rows), slice(h * lanes, (h + 1) * lanes))
                pick_f[at] = jnp.where(hit, 1.0, 0.0)
                prob_f[at] = jnp.where(hit, prob_v[h, e:e + 1, :], 0.0)
        pick_b[...] = pick_f[...].astype(BF16)

    def select(p):
        x = ag[p].reshape(zn * tn, w)
        got = dot(pick_b[...], x, NN)
        if p >= HALF:
            got = got * jnp.sum(prob_f[...], axis=1, keepdims=True)
        send[p] = got.reshape(slots // 8, 8, w).astype(BF16).reshape(en, rows // 8, 8, w)

    def fan_out(src, dst, p, ssem, rsem, osem):
        pltpu.make_async_copy(src.at[p, c], dst.at[p, c], osem.at[p]).start()

        def one(d, carry):
            to = lax.rem(c + d, en)
            pltpu.make_async_remote_copy(
                src_ref=src.at[p, to], dst_ref=dst.at[p, c], send_sem=ssem.at[p], recv_sem=rsem.at[p],
                device_id={"exp": to}, device_id_type=MESH).start()
            return carry

        lax.fori_loop(1, en, one, 0)

    def fan_wait(buf, p, sem):
        pltpu.make_async_copy(
            buf.at[p, pl.ds(0, en - 1)], buf.at[p, pl.ds(0, en - 1)], sem.at[p]).wait()

    def fan_recv(dst, p, rsem, osem):
        fan_wait(dst, p, rsem)
        pltpu.make_async_copy(dst.at[p, 0], dst.at[p, 0], osem.at[p]).wait()

    def flat(ref, p):
        return ref[p].astype(F32).reshape(slots, w).astype(BF16)

    for t in range(PIECES + long):
        if t < PIECES:
            ring_step(t, 0)
        for s in range(1, long):
            if 0 <= t - s < PIECES:
                ring_step(t - s, s)
        if t == 0:
            for copy in weights_out():
                copy.start()
            tables()
        p = t - long
        if 0 <= p < PIECES:
            for way in (0, 1):
                if hops(p, way) > 0:
                    ring_recv(p, way, hops(p, way) - 1)
            select(p)
            fan_out(send, recv, p, d_ssem, d_rsem, own_sem)

    pick_t[...] = pick_f[...].T.astype(BF16)
    prob_t = prob_f[...].T
    hi_t[...] = prob_t.astype(BF16)
    lo_t[...] = (prob_t - prob_t.astype(BF16).astype(F32)).astype(BF16)

    for copy in w_local:
        copy.wait()
    for copy in weights_out():
        copy.wait_recv()

    gate[...] = jnp.zeros_like(gate)
    up[...] = jnp.zeros_like(up)
    dh[...] = jnp.zeros_like(dh)

    def take_tokens(p, carry):
        fan_recv(recv, p, d_rsem, own_sem)
        x = flat(recv, p)
        gate[...] += dot(x, wg_v[p], NN)
        up[...] += dot(x, wu_v[p], NN)
        return carry

    lax.fori_loop(0, HALF, take_tokens, 0)
    chunk = slots // 8

    def forward(i, carry):
        at = pl.ds(pl.multiple_of(i * chunk, chunk), chunk)
        g = gate[at, :]
        hid[at, :] = (g * jax.nn.sigmoid(g) * up[at, :]).astype(BF16)
        return carry

    lax.fori_loop(0, 8, forward, 0)

    def give_out(p, carry):
        y = dot(hid[...], wd_v[p], NN)
        back[p] = y.reshape(slots // 8, 8, w).astype(BF16).reshape(en, rows // 8, 8, w)
        fan_out(back, ret, p, b_ssem, b_rsem, bown_sem)
        return carry

    lax.fori_loop(0, HALF, give_out, 0)

    def take_cot(q, carry):
        p = q + HALF
        fan_recv(recv, p, d_rsem, own_sem)
        dh[...] += dot(flat(recv, p), wd_v[q], NT)
        return carry

    lax.fori_loop(0, HALF, take_cot, 0)

    def backward(i, carry):
        at = pl.ds(pl.multiple_of(i * chunk, chunk), chunk)
        g = gate[at, :]
        sig = jax.nn.sigmoid(g)
        d = dh[at, :]
        dgu[at, :ff] = (d * up[at, :] * sig * (1.0 + g * (1.0 - sig))).astype(BF16)
        dgu[at, ff:] = (d * (g * sig)).astype(BF16)
        return carry

    lax.fori_loop(0, 8, backward, 0)

    def give_grad(q, carry):
        p = q + HALF
        x = dot(dgu[:, :ff], wg_v[q], NT) + dot(dgu[:, ff:], wu_v[q], NT)
        back[p] = x.reshape(slots // 8, 8, w).astype(BF16).reshape(en, rows // 8, 8, w)
        fan_out(back, ret, p, b_ssem, b_rsem, bown_sem)
        return carry

    lax.fori_loop(0, HALF, give_grad, 0)

    def partial_gu(dst, half):
        def one(i, carry):
            dst[i] = dot(flat(recv, half * wq + i), dgu[...], TN).astype(BF16)
            return carry

        lax.fori_loop(0, wq, one, 0)

    def partial_d(dst, half):
        def one(q, carry):
            part_hid = hid[:, pl.ds(pl.multiple_of(half * fh, fh), fh)]
            dst[q] = dot(part_hid, flat(recv, q + HALF), TN).astype(BF16)
            return carry

        lax.fori_loop(0, HALF, one, 0)

    def grads_out():
        return [
            pltpu.make_async_remote_copy(
                src_ref=snd_gu, dst_ref=rcv_gu, send_sem=g_ssem.at[0], recv_sem=g_rsem.at[0],
                device_id={"rep": o}, device_id_type=MESH),
            pltpu.make_async_remote_copy(
                src_ref=snd_d, dst_ref=rcv_d, send_sem=g_ssem.at[1], recv_sem=g_rsem.at[1],
                device_id={"rep": o}, device_id_type=MESH),
        ]

    partial_gu(snd_gu, o)
    grads_out()[0].start()
    partial_d(snd_d, o)
    grads_out()[1].start()
    partial_gu(own_gu, r)
    partial_d(own_d, r)

    def combine(p):
        fan_recv(ret, p, b_rsem, bown_sem)
        x = flat(ret, p)
        if p < HALF:
            total = dot(hi_t[...], x, NN) + dot(lo_t[...], x, NN)
        else:
            total = dot(pick_t[...], x, NN)
        part[p] = total.reshape(zn, tn, w)

    def rs_send(p, way, s):
        return pltpu.make_async_remote_copy(
            src_ref=rs_s.at[way, p, s], dst_ref=rs_r.at[way, p, s],
            send_sem=rs_ssem.at[way, p, s], recv_sem=rs_rsem.at[way, p, s],
            device_id=there(way), device_id_type=MESH)

    def rs_step(p, s):
        for way in (0, 1):
            n = hops(p, way)
            if s < n:
                block = lax.rem(z + step(way) * (n - s) + zn, zn)
                value = part[p, block]
                if s > 0:
                    rs_send(p, way, s - 1).wait_recv()
                    value = value + rs_r[way, p, s - 1].astype(F32)
                rs_s[way, p, s] = value.astype(BF16)
                rs_send(p, way, s).start()

    def rs_final(p):
        value = part[p, z]
        for way in (0, 1):
            n = hops(p, way)
            if n > 0:
                rs_send(p, way, n - 1).wait_recv()
                value = value + rs_r[way, p, n - 1].astype(F32)
        dst = y_v if p < HALF else dx_v
        q = p % HALF
        dst[:, q * w:(q + 1) * w] = value.astype(BF16)

    def finish_gu(i, carry):
        own_gu[i] = (own_gu[i].astype(F32) + rcv_gu[i].astype(F32)).astype(BF16)
        return carry

    def finish_d(i, carry):
        own_d[i] = (own_d[i].astype(F32) + rcv_d[i].astype(F32)).astype(BF16)
        return carry

    def results():
        copies = [
            pltpu.make_async_copy(own_gu.at[:, :, pl.ds(0, ff)], out_g, o_sem.at[0]),
            pltpu.make_async_copy(own_gu.at[:, :, pl.ds(ff, ff)], out_u, o_sem.at[1]),
        ]
        for q in range(HALF):
            copies.append(pltpu.make_async_copy(
                own_d.at[q], out_d.at[:, pl.ds(q * w, w)], o_sem.at[2 + q]))
        return copies

    for t in range(PIECES + long + 1):
        if t < PIECES:
            combine(t)
            rs_step(t, 0)
        for s in range(1, long):
            if 0 <= t - s < PIECES:
                rs_step(t - s, s)
        if 0 <= t - long < PIECES:
            rs_final(t - long)
        if t == HALF - 1:
            for copy in grads_out():
                copy.wait_recv()
            lax.fori_loop(0, wq, finish_gu, 0)
            lax.fori_loop(0, HALF, finish_d, 0)
            for copy in results():
                copy.start()

    last = [
        pltpu.make_async_copy(y_v, out_y, o_sem.at[2 + HALF]),
        pltpu.make_async_copy(dx_v, out_dx, o_sem.at[3 + HALF]),
    ]
    for copy in last:
        copy.start()

    pltpu.make_async_copy(meta_v.at[pl.ds(0, zn - 1)], meta_v.at[pl.ds(0, zn - 1)], m_ssem).wait()
    for copy in weights_out() + grads_out():
        copy.wait_send()
    for p in range(PIECES):
        for way in (0, 1):
            for s in range(hops(p, way)):
                ring(p, way, s).wait_send()
                rs_send(p, way, s).wait_send()
        fan_wait(send, p, d_ssem)
        fan_wait(back, p, b_ssem)
    for copy in results() + last:
        copy.wait()


def local(zn, en, tokens, cotangent, expert_ids, gate_probs, gate_weight, up_weight, down_weight):
    tn, d = tokens.shape
    ff = gate_weight.shape[2]
    w = d // HALF
    wq = HALF // 2
    fh = ff // 2
    rows = RANKS * zn
    slots = en * rows
    lanes = 128
    per = lanes // tn
    long = zn // 2
    z = lax.axis_index("grp")
    table = jnp.concatenate([expert_ids.astype(F32), gate_probs], axis=1).T
    spot = jnp.arange(lanes, dtype=jnp.int32)[None, :] // tn == lax.rem(z, per)
    meta = jnp.where(spot, jnp.tile(table, (1, per)), 0.0)
    vm = pltpu.VMEM
    dma = pltpu.SemaphoreType.DMA
    group = (PIECES, en, rows // 8, 8, w)
    scratch = [
        vm((PIECES, zn, tn, w), BF16),
        vm((zn, 16, lanes), F32),
        vm((HALF, w, ff), BF16),
        vm((HALF, w, ff), BF16),
        vm((HALF, ff, w), BF16),
        vm((zn // per, en, lanes), F32),
        vm((zn // per, en, lanes), F32),
        vm((slots, zn * tn), F32),
        vm((slots, zn * tn), F32),
        vm((slots, zn * tn), BF16),
        vm((zn * tn, slots), BF16),
        vm((zn * tn, slots), BF16),
        vm((zn * tn, slots), BF16),
        vm(group, BF16),
        vm(group, BF16),
        vm((slots, ff), F32),
        vm((slots, ff), F32),
        vm((slots, ff), F32),
        vm((slots, ff), BF16),
        vm((slots, 2 * ff), BF16),
        vm(group, BF16),
        vm(group, BF16),
        vm((PIECES, zn, tn, w), F32),
        vm((2, PIECES, long, tn, w), BF16),
        vm((2, PIECES, long, tn, w), BF16),
        vm((wq, w, 2 * ff), BF16),
        vm((HALF, fh, w), BF16),
        vm((wq, w, 2 * ff), BF16),
        vm((HALF, fh, w), BF16),
        vm((wq, w, 2 * ff), BF16),
        vm((HALF, fh, w), BF16),
        vm((tn, d), BF16),
        vm((tn, d), BF16),
        dma((PIECES,)), dma, dma((2 + HALF,)), dma, dma, dma((2 + HALF,)), dma((2 + HALF,)),
        dma((2, PIECES, long)), dma((2, PIECES, long)), dma((PIECES,)), dma((PIECES,)), dma((PIECES,)),
        dma((PIECES,)), dma((PIECES,)), dma((PIECES,)), dma((2, PIECES, long)), dma((2, PIECES, long)),
        dma((2,)), dma((2,)), dma((4 + HALF,)),
    ]
    hbm = pl.BlockSpec(memory_space=pl.ANY)
    y, dx, g, u, dd = pl.pallas_call(
        functools.partial(kernel, zn, en),
        out_shape=(
            jax.ShapeDtypeStruct((tn, d), BF16),
            jax.ShapeDtypeStruct((tn, d), BF16),
            jax.ShapeDtypeStruct((wq, w, ff), BF16),
            jax.ShapeDtypeStruct((wq, w, ff), BF16),
            jax.ShapeDtypeStruct((fh, d), BF16),
        ),
        in_specs=[hbm] * 6,
        out_specs=(hbm,) * 5,
        scratch_shapes=scratch,
        name="moe",
        compiler_params=pltpu.CompilerParams(
            collective_id=0, has_side_effects=True, vmem_limit_bytes=67043328),
    )(
        tokens, cotangent, meta,
        gate_weight.reshape(wq, w, ff), up_weight.reshape(wq, w, ff), down_weight.reshape(fh, d),
    )
    return y, dx, g.reshape(1, wq * w, ff), u.reshape(1, wq * w, ff), dd.reshape(1, fh, d)


def solution(mesh):
    tokens = P(("grp", "exp", "rep"), None)
    weight = P(("grp", "exp"), "rep", None)
    return jax.shard_map(
        functools.partial(local, mesh.shape["grp"], mesh.shape["exp"]),
        mesh=mesh,
        in_specs=(tokens,) * 4 + (weight,) * 3,
        out_specs=(tokens,) * 2 + (weight,) * 3,
        check_vma=False,
    )
```

```python
import functools

import jax
import jax.numpy as jnp
from jax import lax
from jax.experimental import pallas as pl
from jax.experimental.pallas import tpu as pltpu
from jax.sharding import PartitionSpec as P

MESH = pl.DeviceIdType.MESH
F32 = jnp.float32
BF16 = jnp.bfloat16
RANKS = 3
HALF = 4
PIECES = 2 * HALF


def dot(a, b, dims):
    return lax.dot_general(a, b, (dims, ((), ())), preferred_element_type=F32)


NN = ((1,), (0,))
NT = ((1,), (1,))
TN = ((0,), (0,))


def kernel(
    zn, en,
    ids, prob, tok, cot, wg, wu, wd,
    out_y, out_dx, out_g, out_u, out_d,
    ag, meta_v, wg_v, wu_v, wd_v, rank_v, prob_v, pick_f, prob_f, pick_b, pick_t, hi_t, lo_t,
    send, recv, gate, up, dh, hid, dgu, back, ret, part, rs_s, rs_r, snd_gu, snd_d, rcv_gu, rcv_d,
    l_sem, lw_sem, m_ssem, m_rsem, w_ssem, w_rsem, ag_ssem, ag_rsem, d_ssem, d_rsem, own_sem,
    b_ssem, b_rsem, bown_sem, rs_ssem, rs_rsem, g_ssem, g_rsem,
):
    z = lax.axis_index("grp")
    c = lax.axis_index("exp")
    r = lax.axis_index("rep")
    o = 1 - r
    tn = ag.shape[2]
    w = ag.shape[3]
    rows = RANKS * zn
    slots = en * rows
    ff = gate.shape[1]
    fh = ff // 2
    lanes = 128
    per = lanes // tn
    long = zn // 2

    def hops(p, way):
        return long if (p % 2) == way else zn - 1 - long

    def step(way):
        return 1 if way == 0 else -1

    def there(way):
        return {"grp": lax.rem(z + step(way) + zn, zn)}

    barrier = pltpu.get_barrier_semaphore()
    pl.semaphore_signal(barrier, inc=1, device_id={"rep": o}, device_id_type=MESH)

    def greet_grp(d, carry):
        pl.semaphore_signal(barrier, inc=1, device_id={"grp": lax.rem(z + d, zn)}, device_id_type=MESH)
        return carry

    def greet_exp(d, carry):
        pl.semaphore_signal(barrier, inc=1, device_id={"exp": lax.rem(c + d, en)}, device_id_type=MESH)
        return carry

    lax.fori_loop(1, zn, greet_grp, 0)
    lax.fori_loop(1, en, greet_exp, 0)

    def local(p):
        src = tok if p < HALF else cot
        return pltpu.make_async_copy(
            src.at[:, pl.ds((p % HALF) * w, w)], ag.at[p, z], l_sem.at[p])

    for p in range(PIECES):
        local(p).start()
    wq = HALF // 2
    half_gate = pl.ds(r * wq, wq)
    half_down = pl.ds(pl.multiple_of(r * fh, fh), fh)
    w_local = [
        pltpu.make_async_copy(wg, wg_v.at[half_gate], lw_sem.at[0]),
        pltpu.make_async_copy(wu, wu_v.at[half_gate], lw_sem.at[1]),
    ]
    for q in range(HALF):
        w_local.append(pltpu.make_async_copy(
            wd.at[:, pl.ds(q * w, w)], wd_v.at[q, half_down], lw_sem.at[2 + q]))
    for copy in w_local:
        copy.start()

    lane = lax.broadcasted_iota(jnp.int32, (tn, lanes), 1)
    token = lax.broadcasted_iota(jnp.int32, (tn, lanes), 0)
    spot = ((lane % tn == token) & (lane // tn == lax.rem(z, per))).astype(F32)
    for i, table in enumerate((ids[...].astype(F32), prob[...])):
        meta_v[z, 8 * i:8 * i + 8, :] = lax.dot_general(
            table, spot, (NN, ((), ())), precision=lax.Precision.HIGHEST, preferred_element_type=F32)
    pl.semaphore_wait(barrier, 1 + (zn - 1) + (en - 1))


    def send_meta(d, carry):
        pltpu.make_async_remote_copy(
            src_ref=meta_v.at[z], dst_ref=meta_v.at[z], send_sem=m_ssem, recv_sem=m_rsem,
            device_id={"grp": lax.rem(z + d, zn)}, device_id_type=MESH).start()
        return carry

    lax.fori_loop(1, zn, send_meta, 0)

    def ring(p, way, s):
        block = lax.rem(z - step(way) * s + zn, zn)
        return pltpu.make_async_remote_copy(
            src_ref=ag.at[p, block], dst_ref=ag.at[p, block],
            send_sem=ag_ssem.at[way, p, s], recv_sem=ag_rsem.at[way, p, s],
            device_id=there(way), device_id_type=MESH)

    def ring_recv(p, way, s):
        pltpu.make_async_copy(ag.at[p, 0], ag.at[p, 0], ag_rsem.at[way, p, s]).wait()

    def ring_step(p, s):
        if s == 0:
            local(p).wait()
        for way in (0, 1):
            if s < hops(p, way):
                if s > 0:
                    ring_recv(p, way, s - 1)
                ring(p, way, s).start()

    def weights_out():
        copies = [
            pltpu.make_async_remote_copy(
                src_ref=wg, dst_ref=wg_v.at[half_gate], send_sem=w_ssem.at[0], recv_sem=w_rsem.at[0],
                device_id={"rep": o}, device_id_type=MESH),
            pltpu.make_async_remote_copy(
                src_ref=wu, dst_ref=wu_v.at[half_gate], send_sem=w_ssem.at[1], recv_sem=w_rsem.at[1],
                device_id={"rep": o}, device_id_type=MESH),
        ]
        for q in range(HALF):
            copies.append(pltpu.make_async_remote_copy(
                src_ref=wd.at[:, pl.ds(q * w, w)], dst_ref=wd_v.at[q, half_down],
                send_sem=w_ssem.at[2 + q], recv_sem=w_rsem.at[2 + q],
                device_id={"rep": o}, device_id_type=MESH))
        return copies

    def tables():
        pltpu.make_async_copy(
            meta_v.at[pl.ds(0, zn - 1)], meta_v.at[pl.ds(0, zn - 1)], m_rsem).wait()
        row = lax.broadcasted_iota(jnp.int32, (lanes, lanes), 0)
        col = lax.broadcasted_iota(jnp.int32, (lanes, lanes), 1)
        before = ((row < col) & (row // tn == col // tn)).astype(F32).astype(BF16)
        mine = (lax.broadcasted_iota(jnp.int32, (en, lanes), 0) + en * z).astype(F32)
        sub = lax.broadcasted_iota(jnp.int32, (rows, lanes), 0)
        lane = lax.broadcasted_iota(jnp.int32, (rows, lanes), 1)
        want = (sub // zn).astype(F32)
        for h in range(zn // per):
            both = meta_v[h * per]
            for b in range(1, per):
                both = both + meta_v[h * per + b]
            named = jnp.zeros((en, lanes), F32)
            prob = jnp.zeros((en, lanes), F32)
            for k in range(8):
                hit = both[k:k + 1, :] == mine
                named = named + jnp.where(hit, 1.0, 0.0)
                prob = prob + jnp.where(hit, both[8 + k:9 + k, :], 0.0)
            rank = dot(named.astype(BF16), before, NN)
            rank_v[h] = jnp.where(named > 0.0, rank, -1.0)
            prob_v[h] = prob
            here = (sub % zn) == (h * per + lane // tn)
            for e in range(en):
                hit = (rank_v[h, e:e + 1, :] == want) & here
                at = (slice(e * rows, (e + 1) * rows), slice(h * lanes, (h + 1) * lanes))
                pick_f[at] = jnp.where(hit, 1.0, 0.0)
                prob_f[at] = jnp.where(hit, prob_v[h, e:e + 1, :], 0.0)
        pick_b[...] = pick_f[...].astype(BF16)

    def select(p):
        x = ag[p].reshape(zn * tn, w)
        got = dot(pick_b[...], x, NN)
        if p >= HALF:
            got = got * jnp.sum(prob_f[...], axis=1, keepdims=True)
        send[p] = got.reshape(slots // 8, 8, w).astype(BF16).reshape(en, rows // 8, 8, w)

    def fan_out(src, dst, p, ssem, rsem, osem):
        pltpu.make_async_copy(src.at[p, c], dst.at[p, c], osem.at[p]).start()

        def one(d, carry):
            to = lax.rem(c + d, en)
            pltpu.make_async_remote_copy(
                src_ref=src.at[p, to], dst_ref=dst.at[p, c], send_sem=ssem.at[p], recv_sem=rsem.at[p],
                device_id={"exp": to}, device_id_type=MESH).start()
            return carry

        lax.fori_loop(1, en, one, 0)

    def fan_wait(buf, p, sem):
        pltpu.make_async_copy(
            buf.at[p, pl.ds(0, en - 1)], buf.at[p, pl.ds(0, en - 1)], sem.at[p]).wait()

    def fan_recv(dst, p, rsem, osem):
        fan_wait(dst, p, rsem)
        pltpu.make_async_copy(dst.at[p, 0], dst.at[p, 0], osem.at[p]).wait()

    def flat(ref, p):
        return ref[p].astype(F32).reshape(slots, w).astype(BF16)

    for t in range(PIECES + long):
        p = t - long
        if p == 0:
            tables()
        if p >= 0:
            for way in (0, 1):
                ring_recv(p, way, hops(p, way) - 1)
            select(p)
            fan_out(send, recv, p, d_ssem, d_rsem, own_sem)
        for s in range(long - 1, -1, -1):
            if 0 <= t - s < PIECES:
                ring_step(t - s, s)
        if t == 0:
            for copy in weights_out():
                copy.start()

    pick_t[...] = pick_f[...].T.astype(BF16)
    prob_t = prob_f[...].T
    hi_t[...] = prob_t.astype(BF16)
    lo_t[...] = (prob_t - prob_t.astype(BF16).astype(F32)).astype(BF16)

    for copy in w_local:
        copy.wait()
    for copy in weights_out():
        copy.wait_recv()

    gate[...] = jnp.zeros_like(gate)
    up[...] = jnp.zeros_like(up)
    dh[...] = jnp.zeros_like(dh)

    def take_tokens(p, carry):
        fan_recv(recv, p, d_rsem, own_sem)
        x = flat(recv, p)
        gate[...] += dot(x, wg_v[p], NN)
        up[...] += dot(x, wu_v[p], NN)
        return carry

    lax.fori_loop(0, HALF, take_tokens, 0)
    chunk = slots // 8

    def forward(i, carry):
        at = pl.ds(pl.multiple_of(i * chunk, chunk), chunk)
        g = gate[at, :]
        hid[at, :] = (g * jax.nn.sigmoid(g) * up[at, :]).astype(BF16)
        return carry

    lax.fori_loop(0, 8, forward, 0)

    def give_out(p, carry):
        y = dot(hid[...], wd_v[p], NN)
        back[p] = y.reshape(slots // 8, 8, w).astype(BF16).reshape(en, rows // 8, 8, w)
        fan_out(back, ret, p, b_ssem, b_rsem, bown_sem)
        return carry

    lax.fori_loop(0, HALF, give_out, 0)

    def take_cot(q, carry):
        p = q + HALF
        fan_recv(recv, p, d_rsem, own_sem)
        dh[...] += dot(flat(recv, p), wd_v[q], NT)
        return carry

    lax.fori_loop(0, HALF, take_cot, 0)

    def backward(i, carry):
        at = pl.ds(pl.multiple_of(i * chunk, chunk), chunk)
        g = gate[at, :]
        sig = jax.nn.sigmoid(g)
        d = dh[at, :]
        dgu[at, :ff] = (d * up[at, :] * sig * (1.0 + g * (1.0 - sig))).astype(BF16)
        dgu[at, ff:] = (d * (g * sig)).astype(BF16)
        return carry

    lax.fori_loop(0, 8, backward, 0)

    def give_grad(q, carry):
        p = q + HALF
        x = dot(dgu[:, :ff], wg_v[q], NT) + dot(dgu[:, ff:], wu_v[q], NT)
        back[p] = x.reshape(slots // 8, 8, w).astype(BF16).reshape(en, rows // 8, 8, w)
        fan_out(back, ret, p, b_ssem, b_rsem, bown_sem)
        return carry

    lax.fori_loop(0, HALF, give_grad, 0)

    def partial_gu(i, half):
        return dot(flat(recv, half * wq + i), dgu[...], TN).astype(BF16)

    def partial_d(q, half):
        part_hid = hid[:, pl.ds(pl.multiple_of(half * fh, fh), fh)]
        return dot(part_hid, flat(recv, q + HALF), TN).astype(BF16)

    def columns(q):
        return pl.ds(pl.multiple_of(q * w, w), w)

    def other_gu(i, carry):
        snd_gu[i] = partial_gu(i, o)
        return carry

    def other_d(q, carry):
        snd_d[q] = partial_d(q, o)
        return carry

    def own_gu(i, carry):
        both = partial_gu(i, r)
        out_g[i] = both[:, :ff]
        out_u[i] = both[:, ff:]
        return carry

    def own_d(q, carry):
        out_d[:, columns(q)] = partial_d(q, r)
        return carry

    def grads_out():
        return [
            pltpu.make_async_remote_copy(
                src_ref=snd_gu, dst_ref=rcv_gu, send_sem=g_ssem.at[0], recv_sem=g_rsem.at[0],
                device_id={"rep": o}, device_id_type=MESH),
            pltpu.make_async_remote_copy(
                src_ref=snd_d, dst_ref=rcv_d, send_sem=g_ssem.at[1], recv_sem=g_rsem.at[1],
                device_id={"rep": o}, device_id_type=MESH),
        ]

    def combine(p):
        fan_recv(ret, p, b_rsem, bown_sem)
        x = flat(ret, p)
        if p < HALF:
            total = dot(hi_t[...], x, NN) + dot(lo_t[...], x, NN)
        else:
            total = dot(pick_t[...], x, NN)
        part[p] = total.reshape(zn, tn, w)

    def rs_send(p, way, s):
        return pltpu.make_async_remote_copy(
            src_ref=rs_s.at[way, p, s], dst_ref=rs_r.at[way, p, s],
            send_sem=rs_ssem.at[way, p, s], recv_sem=rs_rsem.at[way, p, s],
            device_id=there(way), device_id_type=MESH)

    def rs_step(p, s):
        for way in (0, 1):
            n = hops(p, way)
            if s < n:
                block = lax.rem(z + step(way) * (n - s) + zn, zn)
                value = part[p, block]
                if s > 0:
                    rs_send(p, way, s - 1).wait_recv()
                    value = value + rs_r[way, p, s - 1].astype(F32)
                rs_s[way, p, s] = value.astype(BF16)
                rs_send(p, way, s).start()

    def rs_final(p):
        value = part[p, z]
        for way in (0, 1):
            n = hops(p, way)
            rs_send(p, way, n - 1).wait_recv()
            value = value + rs_r[way, p, n - 1].astype(F32)
        dst = out_y if p < HALF else out_dx
        q = p % HALF
        dst[:, q * w:(q + 1) * w] = value.astype(BF16)

    def finish_gu(i, carry):
        out_g[i] = (out_g[i].astype(F32) + rcv_gu[i, :, :ff].astype(F32)).astype(BF16)
        out_u[i] = (out_u[i].astype(F32) + rcv_gu[i, :, ff:].astype(F32)).astype(BF16)
        return carry

    def finish_d(q, carry):
        out_d[:, columns(q)] = (out_d[:, columns(q)].astype(F32) + rcv_d[q].astype(F32)).astype(BF16)
        return carry

    def fill(t):
        if t < wq:
            other_gu(t, 0)
            if t == wq - 1:
                grads_out()[0].start()
        elif t == wq:
            lax.fori_loop(0, HALF, other_d, 0)
            grads_out()[1].start()
        elif t < 2 * wq + 1:
            own_gu(t - wq - 1, 0)
        elif t == 2 * wq + 1:
            lax.fori_loop(0, HALF, own_d, 0)
        elif t == 2 * wq + 2:
            for copy in grads_out():
                copy.wait_recv()
            lax.fori_loop(0, wq, finish_gu, 0)
            lax.fori_loop(0, HALF, finish_d, 0)
        elif t == 2 * wq + 3:
            pltpu.make_async_copy(
                meta_v.at[pl.ds(0, zn - 1)], meta_v.at[pl.ds(0, zn - 1)], m_ssem).wait()
            for copy in weights_out() + grads_out():
                copy.wait_send()
            for p in range(PIECES):
                for way in (0, 1):
                    for s in range(hops(p, way)):
                        ring(p, way, s).wait_send()
            for p in range(PIECES):
                fan_wait(send, p, d_ssem)
                fan_wait(back, p, b_ssem)

    for t in range(PIECES + long + 1):
        for s in range(long - 1, 0, -1):
            if 0 <= t - s - 1 < PIECES:
                rs_step(t - s - 1, s)
        if t < PIECES:
            combine(t)
            rs_step(t, 0)
        if t > long:
            rs_final(t - long - 1)
        fill(t)

    for p in range(PIECES):
        for way in (0, 1):
            for s in range(hops(p, way)):
                rs_send(p, way, s).wait_send()


def local(zn, en, tokens, cotangent, expert_ids, gate_probs, gate_weight, up_weight, down_weight):
    tn, d = tokens.shape
    ff = gate_weight.shape[2]
    w = d // HALF
    wq = HALF // 2
    fh = ff // 2
    rows = RANKS * zn
    slots = en * rows
    lanes = 128
    per = lanes // tn
    long = zn // 2
    vm = pltpu.VMEM
    dma = pltpu.SemaphoreType.DMA
    group = (PIECES, en, rows // 8, 8, w)
    scratch = [
        vm((PIECES, zn, tn, w), BF16),
        vm((zn, 16, lanes), F32),
        vm((HALF, w, ff), BF16),
        vm((HALF, w, ff), BF16),
        vm((HALF, ff, w), BF16),
        vm((zn // per, en, lanes), F32),
        vm((zn // per, en, lanes), F32),
        vm((slots, zn * tn), F32),
        vm((slots, zn * tn), F32),
        vm((slots, zn * tn), BF16),
        vm((zn * tn, slots), BF16),
        vm((zn * tn, slots), BF16),
        vm((zn * tn, slots), BF16),
        vm(group, BF16),
        vm(group, BF16),
        vm((slots, ff), F32),
        vm((slots, ff), F32),
        vm((slots, ff), F32),
        vm((slots, ff), BF16),
        vm((slots, 2 * ff), BF16),
        vm(group, BF16),
        vm(group, BF16),
        vm((PIECES, zn, tn, w), F32),
        vm((2, PIECES, long, tn, w), BF16),
        vm((2, PIECES, long, tn, w), BF16),
        vm((wq, w, 2 * ff), BF16),
        vm((HALF, fh, w), BF16),
        vm((wq, w, 2 * ff), BF16),
        vm((HALF, fh, w), BF16),
        dma((PIECES,)), dma((2 + HALF,)), dma, dma, dma((2 + HALF,)), dma((2 + HALF,)),
        dma((2, PIECES, long)), dma((2, PIECES, long)), dma((PIECES,)), dma((PIECES,)), dma((PIECES,)),
        dma((PIECES,)), dma((PIECES,)), dma((PIECES,)), dma((2, PIECES, long)), dma((2, PIECES, long)),
        dma((2,)), dma((2,)),
    ]
    hbm = pl.BlockSpec(memory_space=pl.ANY)
    y, dx, g, u, dd = pl.pallas_call(
        functools.partial(kernel, zn, en),
        out_shape=(
            pltpu.VMEM((tn, d), BF16),
            pltpu.VMEM((tn, d), BF16),
            pltpu.VMEM((wq, w, ff), BF16),
            pltpu.VMEM((wq, w, ff), BF16),
            pltpu.VMEM((fh, d), BF16),
        ),
        in_specs=[pl.BlockSpec(memory_space=pltpu.VMEM)] * 2 + [hbm] * 5,
        out_specs=(pl.BlockSpec(memory_space=pltpu.VMEM),) * 5,
        scratch_shapes=scratch,
        name="moe",
        compiler_params=pltpu.CompilerParams(
            collective_id=0, has_side_effects=True, vmem_limit_bytes=58000000),
    )(
        expert_ids.T, gate_probs.T, tokens, cotangent,
        gate_weight.reshape(wq, w, ff), up_weight.reshape(wq, w, ff), down_weight.reshape(fh, d),
    )
    return y, dx, g.reshape(1, wq * w, ff), u.reshape(1, wq * w, ff), dd.reshape(1, fh, d)


def solution(mesh):
    tokens = P(("grp", "exp", "rep"), None)
    weight = P(("grp", "exp"), "rep", None)
    return jax.shard_map(
        functools.partial(local, mesh.shape["grp"], mesh.shape["exp"]),
        mesh=mesh,
        in_specs=(tokens,) * 4 + (weight,) * 3,
        out_specs=(tokens,) * 2 + (weight,) * 3,
        check_vma=False,
    )
```

```python
import functools

import jax
import jax.numpy as jnp
from jax import lax
from jax.experimental import pallas as pl
from jax.experimental.pallas import tpu as pltpu
from jax.sharding import PartitionSpec as P

MESH = pl.DeviceIdType.MESH
F32 = jnp.float32
BF16 = jnp.bfloat16
RANKS = 3
HALF = 4
PIECES = 2 * HALF
CROSS = 2
RING = PIECES - CROSS


def dot(a, b, dims):
    return lax.dot_general(a, b, (dims, ((), ())), preferred_element_type=F32)


NN = ((1,), (0,))
NT = ((1,), (1,))
TN = ((0,), (0,))


def kernel(
    zn, en,
    ids, prob, tok, cot, wg, wu, wd,
    out_y, out_dx, out_g, out_u, out_d,
    ag, meta_v, wg_v, wu_v, wd_v, rank_v, prob_v, pick_f, prob_f, pick_b, pick_t, hi_t, lo_t,
    send, recv, gate, up, dh, hid, dgu, back, ret, part, rs_s, rs_r, snd_gu, snd_d, rcv_gu, rcv_d,
    l_sem, lw_sem, m_ssem, m_rsem, w_ssem, w_rsem, ag_ssem, ag_rsem, d_ssem, d_rsem, own_sem,
    b_ssem, b_rsem, bown_sem, rs_ssem, rs_rsem, g_ssem, g_rsem,
    ids_v, chance_v, all_rank, all_prob, own_f, own_prob, own_pick, own_hi, own_lo, order,
    x_r, z_s, z_r, back_z_s, back_z_r, back_x, ids_sem, x_ssem, x_rsem, x_own, z_ssem, z_rsem, bz_ssem, bz_rsem,
):
    z = lax.axis_index("grp")
    c = lax.axis_index("exp")
    r = lax.axis_index("rep")
    o = 1 - r
    tn = ag.shape[2]
    w = ag.shape[3]
    rows = RANKS * zn
    slots = en * rows
    ff = gate.shape[1]
    fh = ff // 2
    lanes = 128
    per = lanes // tn
    long = zn // 2

    def hops(p, way):
        return long if (p % 2) == way else zn - 1 - long

    def step(way):
        return 1 if way == 0 else -1

    def there(way):
        return {"grp": lax.rem(z + step(way) + zn, zn)}

    barrier = pltpu.get_barrier_semaphore()
    pl.semaphore_signal(barrier, inc=1, device_id={"rep": o}, device_id_type=MESH)

    def greet_grp(d, carry):
        pl.semaphore_signal(barrier, inc=1, device_id={"grp": lax.rem(z + d, zn)}, device_id_type=MESH)
        return carry

    def greet_exp(d, carry):
        pl.semaphore_signal(barrier, inc=1, device_id={"exp": lax.rem(c + d, en)}, device_id_type=MESH)
        return carry

    lax.fori_loop(1, zn, greet_grp, 0)
    lax.fori_loop(1, en, greet_exp, 0)

    def local(p):
        src = tok if p < HALF else cot
        return pltpu.make_async_copy(
            src.at[:, pl.ds((p % HALF) * w, w)], ag.at[p, z], l_sem.at[p])

    tables_in = [
        pltpu.make_async_copy(ids, ids_v, ids_sem.at[0]),
        pltpu.make_async_copy(prob, chance_v, ids_sem.at[1]),
    ]
    for copy in tables_in:
        copy.start()
    for p in list(range(RING, PIECES)) + list(range(RING)):
        local(p).start()
    wq = HALF // 2
    half_gate = pl.ds(r * wq, wq)
    half_down = pl.ds(pl.multiple_of(r * fh, fh), fh)
    w_local = [
        pltpu.make_async_copy(wg, wg_v.at[half_gate], lw_sem.at[0]),
        pltpu.make_async_copy(wu, wu_v.at[half_gate], lw_sem.at[1]),
    ]
    for q in range(HALF):
        w_local.append(pltpu.make_async_copy(
            wd.at[:, pl.ds(q * w, w)], wd_v.at[q, half_down], lw_sem.at[2 + q]))
    for copy in w_local:
        copy.start()

    lane = lax.broadcasted_iota(jnp.int32, (tn, lanes), 1)
    token = lax.broadcasted_iota(jnp.int32, (tn, lanes), 0)
    spot = ((lane % tn == token) & (lane // tn == lax.rem(z, per))).astype(F32)
    for copy in tables_in:
        copy.wait()
    for i, table in enumerate((ids_v[...].astype(F32), chance_v[...])):
        meta_v[z, 8 * i:8 * i + 8, :] = lax.dot_general(
            table, spot, (NN, ((), ())), precision=lax.Precision.HIGHEST, preferred_element_type=F32)

    row = lax.broadcasted_iota(jnp.int32, (lanes, lanes), 0)
    col = lax.broadcasted_iota(jnp.int32, (lanes, lanes), 1)
    before = ((row < col) & (row // tn == col // tn)).astype(F32).astype(BF16)
    expert = lax.broadcasted_iota(jnp.int32, (en * zn, tn), 0).astype(F32)
    named = jnp.zeros((en * zn, tn), F32)
    weight = jnp.zeros((en * zn, tn), F32)
    for k in range(8):
        hit = ids_v[k:k + 1, :].astype(F32) == expert
        named = named + jnp.where(hit, 1.0, 0.0)
        weight = weight + jnp.where(hit, chance_v[k:k + 1, :], 0.0)
    rank = dot(named.astype(BF16), before[:tn, :tn], NN)
    all_rank[...] = jnp.where(named > 0.0, rank, -1.0)
    all_prob[...] = weight
    for e in range(en):
        seen = all_rank[pl.ds(e, zn, stride=en), :]
        worth = all_prob[pl.ds(e, zn, stride=en), :]
        for k in range(RANKS):
            at = slice((e * RANKS + k) * zn, (e * RANKS + k + 1) * zn)
            own_f[at, :] = jnp.where(seen == float(k), 1.0, 0.0)
            own_prob[at, :] = jnp.where(seen == float(k), worth, 0.0)
    own_pick[...] = own_f[...].astype(BF16)
    near = en * RANKS
    row = lax.broadcasted_iota(jnp.int32, (slots, slots), 0)
    col = lax.broadcasted_iota(jnp.int32, (slots, slots), 1)
    order[...] = ((row // near == col % zn) & (row % near == col // zn)).astype(F32).astype(BF16)
    pl.semaphore_wait(barrier, 1 + (zn - 1) + (en - 1))


    def send_meta(d, carry):
        pltpu.make_async_remote_copy(
            src_ref=meta_v.at[z], dst_ref=meta_v.at[z], send_sem=m_ssem, recv_sem=m_rsem,
            device_id={"grp": lax.rem(z + d, zn)}, device_id_type=MESH).start()
        return carry

    lax.fori_loop(1, zn, send_meta, 0)

    def ring(p, way, s):
        block = lax.rem(z - step(way) * s + zn, zn)
        return pltpu.make_async_remote_copy(
            src_ref=ag.at[p, block], dst_ref=ag.at[p, block],
            send_sem=ag_ssem.at[way], recv_sem=ag_rsem.at[way, p, s],
            device_id=there(way), device_id_type=MESH)

    def ring_recv(p, way, s):
        pltpu.make_async_copy(ag.at[p, 0], ag.at[p, 0], ag_rsem.at[way, p, s]).wait()

    def ring_step(p, s):
        if s == 0:
            local(p).wait()
        for way in (0, 1):
            if s < hops(p, way):
                if s > 0:
                    ring_recv(p, way, s - 1)
                ring(p, way, s).start()

    def ring_sent(sem, way):
        some = ag.at[pl.ds(0, RING // 2), pl.ds(0, zn - 1)]
        pltpu.make_async_copy(some, some, sem.at[way]).wait()

    def weights_out():
        copies = [
            pltpu.make_async_remote_copy(
                src_ref=wg, dst_ref=wg_v.at[half_gate], send_sem=w_ssem.at[0], recv_sem=w_rsem.at[0],
                device_id={"rep": o}, device_id_type=MESH),
            pltpu.make_async_remote_copy(
                src_ref=wu, dst_ref=wu_v.at[half_gate], send_sem=w_ssem.at[1], recv_sem=w_rsem.at[1],
                device_id={"rep": o}, device_id_type=MESH),
        ]
        for q in range(HALF):
            copies.append(pltpu.make_async_remote_copy(
                src_ref=wd.at[:, pl.ds(q * w, w)], dst_ref=wd_v.at[q, half_down],
                send_sem=w_ssem.at[2 + q], recv_sem=w_rsem.at[2 + q],
                device_id={"rep": o}, device_id_type=MESH))
        return copies

    def tables():
        pltpu.make_async_copy(
            meta_v.at[pl.ds(0, zn - 1)], meta_v.at[pl.ds(0, zn - 1)], m_rsem).wait()
        row = lax.broadcasted_iota(jnp.int32, (lanes, lanes), 0)
        col = lax.broadcasted_iota(jnp.int32, (lanes, lanes), 1)
        before = ((row < col) & (row // tn == col // tn)).astype(F32).astype(BF16)
        mine = (lax.broadcasted_iota(jnp.int32, (en, lanes), 0) + en * z).astype(F32)
        sub = lax.broadcasted_iota(jnp.int32, (rows, lanes), 0)
        lane = lax.broadcasted_iota(jnp.int32, (rows, lanes), 1)
        want = (sub // zn).astype(F32)
        for h in range(zn // per):
            both = meta_v[h * per]
            for b in range(1, per):
                both = both + meta_v[h * per + b]
            named = jnp.zeros((en, lanes), F32)
            prob = jnp.zeros((en, lanes), F32)
            for k in range(8):
                hit = both[k:k + 1, :] == mine
                named = named + jnp.where(hit, 1.0, 0.0)
                prob = prob + jnp.where(hit, both[8 + k:9 + k, :], 0.0)
            rank = dot(named.astype(BF16), before, NN)
            rank_v[h] = jnp.where(named > 0.0, rank, -1.0)
            prob_v[h] = prob
            here = (sub % zn) == (h * per + lane // tn)
            for e in range(en):
                hit = (rank_v[h, e:e + 1, :] == want) & here
                at = (slice(e * rows, (e + 1) * rows), slice(h * lanes, (h + 1) * lanes))
                pick_f[at] = jnp.where(hit, 1.0, 0.0)
                prob_f[at] = jnp.where(hit, prob_v[h, e:e + 1, :], 0.0)
        pick_b[...] = pick_f[...].astype(BF16)

    def select(p):
        x = ag[p].reshape(zn * tn, w)
        got = dot(pick_b[...], x, NN)
        if p >= HALF:
            got = got * jnp.sum(prob_f[...], axis=1, keepdims=True)
        send[p] = grouped(got)

    def fan_out(src, i, dst, p, ssem, rsem, osem):
        pltpu.make_async_copy(src.at[i, c], dst.at[p, c], osem.at[p]).start()

        def one(d, carry):
            to = lax.rem(c + d, en)
            pltpu.make_async_remote_copy(
                src_ref=src.at[i, to], dst_ref=dst.at[p, c], send_sem=ssem.at[p], recv_sem=rsem.at[p],
                device_id={"exp": to}, device_id_type=MESH).start()
            return carry

        lax.fori_loop(1, en, one, 0)

    def fan_wait(buf, p, sem):
        pltpu.make_async_copy(
            buf.at[0, pl.ds(0, en - 1)], buf.at[0, pl.ds(0, en - 1)], sem.at[p]).wait()

    def fan_recv(dst, p, rsem, osem):
        fan_wait(dst, p, rsem)
        pltpu.make_async_copy(dst.at[p, 0], dst.at[p, 0], osem.at[p]).wait()

    def grouped(value):
        return value.reshape(slots // 8, 8, w).astype(BF16).reshape(en, rows // 8, 8, w)

    def across(src, dst, i, d, ssem, rsem):
        to = lax.rem(z + d, zn)
        pltpu.make_async_remote_copy(
            src_ref=src.at[i, to], dst_ref=dst.at[i, z], send_sem=ssem.at[i], recv_sem=rsem.at[i],
            device_id={"grp": to}, device_id_type=MESH).start()

    def across_wait(buf, i, sem):
        some = buf.at[i, pl.ds(0, zn - 1)]
        pltpu.make_async_copy(some, some, sem.at[i]).wait()

    def by_group(dst, i, value):
        dst[i] = dot(order[...], value, NN).astype(BF16).reshape(zn, near, w)

    def from_groups(src, own, i):
        src[i, z] = own[i, z]
        return dot(order[...], src[i].reshape(slots, w), TN)

    def select_own(i):
        got = dot(own_pick[...], ag[RING + i, z], NN)
        return got * jnp.sum(own_prob[...], axis=1, keepdims=True)

    def flat(ref, p):
        return ref[p].astype(F32).reshape(slots, w).astype(BF16)

    for t in range(RING + long):
        p = t - long
        if p == 0:
            tables()
        if p >= 0:
            for way in (0, 1):
                ring_recv(p, way, hops(p, way) - 1)
            select(p)
            fan_out(send, p, recv, p, d_ssem, d_rsem, own_sem)
        for s in range(long - 1, -1, -1):
            if 0 <= t - s < RING:
                ring_step(t - s, s)
        if t == 0:
            for i in range(CROSS):
                local(RING + i).wait()
                send[RING + i] = grouped(select_own(i))
            for i in range(CROSS):
                fan_out(send, RING + i, x_r, i, x_ssem, x_rsem, x_own)
            for copy in weights_out():
                copy.start()
        for i in range(CROSS):
            if t == long + i:
                fan_recv(x_r, i, x_rsem, x_own)
                by_group(z_s, i, flat(x_r, i))
            for d in sorted({t - long - i, zn - t + long + i}):
                if 0 < t - long - i <= long:
                    across(z_s, z_r, i, d, z_ssem, z_rsem)

    pick_t[...] = pick_f[...].T.astype(BF16)
    prob_t = prob_f[...].T
    hi_t[...] = prob_t.astype(BF16)
    lo_t[...] = (prob_t - prob_t.astype(BF16).astype(F32)).astype(BF16)
    own_t = own_prob[...].T
    own_hi[...] = own_t.astype(BF16)
    own_lo[...] = (own_t - own_t.astype(BF16).astype(F32)).astype(BF16)

    for copy in w_local:
        copy.wait()
    for copy in weights_out():
        copy.wait_recv()

    gate[...] = jnp.zeros_like(gate)
    up[...] = jnp.zeros_like(up)
    dh[...] = jnp.zeros_like(dh)

    def take_tokens(p, carry):
        fan_recv(recv, p, d_rsem, own_sem)
        x = flat(recv, p)
        gate[...] += dot(x, wg_v[p], NN)
        up[...] += dot(x, wu_v[p], NN)
        return carry

    lax.fori_loop(0, HALF, take_tokens, 0)
    chunk = slots // 8

    def forward(i, carry):
        at = pl.ds(pl.multiple_of(i * chunk, chunk), chunk)
        g = gate[at, :]
        hid[at, :] = (g * jax.nn.sigmoid(g) * up[at, :]).astype(BF16)
        return carry

    lax.fori_loop(0, 8, forward, 0)

    def give_out(p, carry):
        y = dot(hid[...], wd_v[p], NN)
        back[p] = grouped(y)
        fan_out(back, p, ret, p, b_ssem, b_rsem, bown_sem)
        return carry

    lax.fori_loop(0, HALF - CROSS, give_out, 0)

    def give_across(i, carry):
        by_group(back_z_s, i, dot(hid[...], wd_v[HALF - CROSS + i], NN).astype(BF16))

        def one(d, inner):
            across(back_z_s, back_z_r, i, d, bz_ssem, bz_rsem)
            return inner

        lax.fori_loop(1, zn, one, 0)
        return carry

    lax.fori_loop(0, CROSS, give_across, 0)

    def take_cot(q, carry):
        p = q + HALF
        fan_recv(recv, p, d_rsem, own_sem)
        dh[...] += dot(flat(recv, p), wd_v[q], NT)
        return carry

    lax.fori_loop(0, HALF - CROSS, take_cot, 0)

    def take_across(i, carry):
        across_wait(z_r, i, z_rsem)
        x = from_groups(z_r, z_s, i)
        recv[RING + i] = grouped(x)
        dh[...] += dot(x.astype(BF16), wd_v[HALF - CROSS + i], NT)
        return carry

    lax.fori_loop(0, CROSS, take_across, 0)

    def backward(i, carry):
        at = pl.ds(pl.multiple_of(i * chunk, chunk), chunk)
        g = gate[at, :]
        sig = jax.nn.sigmoid(g)
        d = dh[at, :]
        dgu[at, :ff] = (d * up[at, :] * sig * (1.0 + g * (1.0 - sig))).astype(BF16)
        dgu[at, ff:] = (d * (g * sig)).astype(BF16)
        return carry

    lax.fori_loop(0, 8, backward, 0)

    def give_grad(q, carry):
        p = q + HALF
        x = dot(dgu[:, :ff], wg_v[q], NT) + dot(dgu[:, ff:], wu_v[q], NT)
        back[p] = grouped(x)
        fan_out(back, p, ret, p, b_ssem, b_rsem, bown_sem)
        return carry

    lax.fori_loop(0, HALF, give_grad, 0)

    def partial_gu(i, half):
        return dot(flat(recv, half * wq + i), dgu[...], TN).astype(BF16)

    def partial_d(q, half):
        part_hid = hid[:, pl.ds(pl.multiple_of(half * fh, fh), fh)]
        return dot(part_hid, flat(recv, q + HALF), TN).astype(BF16)

    def columns(q):
        return pl.ds(pl.multiple_of(q * w, w), w)

    def other_gu(i, carry):
        snd_gu[i] = partial_gu(i, o)
        return carry

    def other_d(q, carry):
        snd_d[q] = partial_d(q, o)
        return carry

    def own_gu(i, carry):
        both = partial_gu(i, r)
        out_g[i] = both[:, :ff]
        out_u[i] = both[:, ff:]
        return carry

    def own_d(q, carry):
        out_d[:, columns(q)] = partial_d(q, r)
        return carry

    def grads_out():
        return [
            pltpu.make_async_remote_copy(
                src_ref=snd_gu, dst_ref=rcv_gu, send_sem=g_ssem.at[0], recv_sem=g_rsem.at[0],
                device_id={"rep": o}, device_id_type=MESH),
            pltpu.make_async_remote_copy(
                src_ref=snd_d, dst_ref=rcv_d, send_sem=g_ssem.at[1], recv_sem=g_rsem.at[1],
                device_id={"rep": o}, device_id_type=MESH),
        ]

    def combine(p):
        fan_recv(ret, p, b_rsem, bown_sem)
        x = flat(ret, p)
        if p < HALF:
            total = dot(hi_t[...], x, NN) + dot(lo_t[...], x, NN)
        else:
            total = dot(pick_t[...], x, NN)
        part[p] = total.reshape(zn, tn, w)

    rings = list(range(HALF - CROSS)) + list(range(HALF, PIECES))

    def rs_send(n, way, s):
        return pltpu.make_async_remote_copy(
            src_ref=rs_s.at[way, n, s], dst_ref=rs_r.at[way, n, s],
            send_sem=rs_ssem.at[way], recv_sem=rs_rsem.at[way, n, s],
            device_id=there(way), device_id_type=MESH)

    def rs_step(n, s):
        for way in (0, 1):
            far = hops(n, way)
            if s < far:
                block = lax.rem(z + step(way) * (far - s) + zn, zn)
                value = part[rings[n], block]
                if s > 0:
                    rs_send(n, way, s - 1).wait_recv()
                    value = value + rs_r[way, n, s - 1].astype(F32)
                rs_s[way, n, s] = value.astype(BF16)
                rs_send(n, way, s).start()

    def put(p, value):
        dst = out_y if p < HALF else out_dx
        q = p % HALF
        dst[:, q * w:(q + 1) * w] = value.astype(BF16)

    def rs_final(n):
        value = part[rings[n], z]
        for way in (0, 1):
            far = hops(n, way)
            rs_send(n, way, far - 1).wait_recv()
            value = value + rs_r[way, n, far - 1].astype(F32)
        put(rings[n], value)

    def turn(i):
        across_wait(back_z_r, i, bz_rsem)
        back_x[i] = grouped(from_groups(back_z_r, back_z_s, i))
        fan_out(back_x, i, ret, HALF - CROSS + i, b_ssem, b_rsem, bown_sem)

    def arrive(i):
        p = HALF - CROSS + i
        fan_recv(ret, p, b_rsem, bown_sem)
        x = flat(ret, p)
        put(p, dot(own_hi[...], x, NN) + dot(own_lo[...], x, NN))

    def finish_gu(i, carry):
        out_g[i] = (out_g[i].astype(F32) + rcv_gu[i, :, :ff].astype(F32)).astype(BF16)
        out_u[i] = (out_u[i].astype(F32) + rcv_gu[i, :, ff:].astype(F32)).astype(BF16)
        return carry

    def finish_d(q, carry):
        out_d[:, columns(q)] = (out_d[:, columns(q)].astype(F32) + rcv_d[q].astype(F32)).astype(BF16)
        return carry

    def fill(t):
        if t < wq:
            other_gu(t, 0)
            if t == wq - 1:
                grads_out()[0].start()
        elif t == wq:
            lax.fori_loop(0, HALF, other_d, 0)
            grads_out()[1].start()
        elif t < 2 * wq + 1:
            own_gu(t - wq - 1, 0)
        elif t == 2 * wq + 1:
            lax.fori_loop(0, HALF, own_d, 0)
        elif t == 2 * wq + 2:
            for copy in grads_out():
                copy.wait_recv()
            lax.fori_loop(0, wq, finish_gu, 0)
            lax.fori_loop(0, HALF, finish_d, 0)
        elif t == 2 * wq + 3:
            pltpu.make_async_copy(
                meta_v.at[pl.ds(0, zn - 1)], meta_v.at[pl.ds(0, zn - 1)], m_ssem).wait()
            for copy in weights_out() + grads_out():
                copy.wait_send()
            for way in (0, 1):
                ring_sent(ag_ssem, way)
            for p in range(RING):
                fan_wait(send, p, d_ssem)
            for p in range(PIECES):
                fan_wait(back, p, b_ssem)
            for i in range(CROSS):
                fan_wait(send, i, x_ssem)
                across_wait(z_s, i, z_ssem)
                across_wait(back_z_s, i, bz_ssem)

    for t in range(RING + long + 1):
        for s in range(long - 1, 0, -1):
            if 0 <= t - s - 1 < RING:
                rs_step(t - s - 1, s)
        if t < RING:
            combine(rings[t])
            rs_step(t, 0)
        if t > long:
            rs_final(t - long - 1)
        fill(t)
        if 0 < t <= CROSS:
            turn(t - 1)
        if RING < t <= RING + CROSS:
            arrive(t - RING - 1)

    for way in (0, 1):
        ring_sent(rs_ssem, way)


def local(zn, en, tokens, cotangent, expert_ids, gate_probs, gate_weight, up_weight, down_weight):
    tn, d = tokens.shape
    ff = gate_weight.shape[2]
    w = d // HALF
    wq = HALF // 2
    fh = ff // 2
    rows = RANKS * zn
    slots = en * rows
    lanes = 128
    per = lanes // tn
    long = zn // 2
    vm = pltpu.VMEM
    dma = pltpu.SemaphoreType.DMA
    group = (PIECES, en, rows // 8, 8, w)
    scratch = [
        vm((PIECES, zn, tn, w), BF16),
        vm((zn, 16, lanes), F32),
        vm((HALF, w, ff), BF16),
        vm((HALF, w, ff), BF16),
        vm((HALF, ff, w), BF16),
        vm((zn // per, en, lanes), F32),
        vm((zn // per, en, lanes), F32),
        vm((slots, zn * tn), F32),
        vm((slots, zn * tn), F32),
        vm((slots, zn * tn), BF16),
        vm((zn * tn, slots), BF16),
        vm((zn * tn, slots), BF16),
        vm((zn * tn, slots), BF16),
        vm(group, BF16),
        vm(group, BF16),
        vm((slots, ff), F32),
        vm((slots, ff), F32),
        vm((slots, ff), F32),
        vm((slots, ff), BF16),
        vm((slots, 2 * ff), BF16),
        vm(group, BF16),
        vm(group, BF16),
        vm((PIECES, zn, tn, w), F32),
        vm((2, RING, long, tn, w), BF16),
        vm((2, RING, long, tn, w), BF16),
        vm((wq, w, 2 * ff), BF16),
        vm((HALF, fh, w), BF16),
        vm((wq, w, 2 * ff), BF16),
        vm((HALF, fh, w), BF16),
        dma((PIECES,)), dma((2 + HALF,)), dma, dma, dma((2 + HALF,)), dma((2 + HALF,)),
        dma((2,)), dma((2, RING, long)), dma((RING,)), dma((RING,)), dma((RING,)),
        dma((PIECES,)), dma((PIECES,)), dma((PIECES,)), dma((2,)), dma((2, RING, long)),
        dma((2,)), dma((2,)),
        vm((8, tn), jnp.int32),
        vm((8, tn), F32),
        vm((en * zn, tn), F32),
        vm((en * zn, tn), F32),
        vm((slots, tn), F32),
        vm((slots, tn), F32),
        vm((slots, tn), BF16),
        vm((tn, slots), BF16),
        vm((tn, slots), BF16),
        vm((slots, slots), BF16),
        vm((CROSS,) + group[1:], BF16),
        vm((CROSS, zn, en * RANKS, w), BF16),
        vm((CROSS, zn, en * RANKS, w), BF16),
        vm((CROSS, zn, en * RANKS, w), BF16),
        vm((CROSS, zn, en * RANKS, w), BF16),
        vm((CROSS,) + group[1:], BF16),
        dma((2,)), dma((CROSS,)), dma((CROSS,)), dma((CROSS,)), dma((CROSS,)), dma((CROSS,)),
        dma((CROSS,)), dma((CROSS,)),
    ]
    hbm = pl.BlockSpec(memory_space=pl.ANY)
    y, dx, g, u, dd = pl.pallas_call(
        functools.partial(kernel, zn, en),
        out_shape=(
            pltpu.VMEM((tn, d), BF16),
            pltpu.VMEM((tn, d), BF16),
            pltpu.VMEM((wq, w, ff), BF16),
            pltpu.VMEM((wq, w, ff), BF16),
            pltpu.VMEM((fh, d), BF16),
        ),
        in_specs=[hbm] * 7,
        out_specs=(pl.BlockSpec(memory_space=pltpu.VMEM),) * 5,
        scratch_shapes=scratch,
        name="moe",
        compiler_params=pltpu.CompilerParams(
            collective_id=0, has_side_effects=True, vmem_limit_bytes=58000000),
    )(
        expert_ids.T, gate_probs.T, tokens, cotangent,
        gate_weight.reshape(wq, w, ff), up_weight.reshape(wq, w, ff), down_weight.reshape(fh, d),
    )
    return y, dx, g.reshape(1, wq * w, ff), u.reshape(1, wq * w, ff), dd.reshape(1, fh, d)


def solution(mesh):
    tokens = P(("grp", "exp", "rep"), None)
    weight = P(("grp", "exp"), "rep", None)
    return jax.shard_map(
        functools.partial(local, mesh.shape["grp"], mesh.shape["exp"]),
        mesh=mesh,
        in_specs=(tokens,) * 4 + (weight,) * 3,
        out_specs=(tokens,) * 2 + (weight,) * 3,
        check_vma=False,
    )
```

```python
import functools

import jax
import jax.numpy as jnp
from jax import lax
from jax.experimental import pallas as pl
from jax.experimental.pallas import tpu as pltpu
from jax.sharding import PartitionSpec as P

MESH = pl.DeviceIdType.MESH
F32 = jnp.float32
BF16 = jnp.bfloat16
RANKS = 3
HALF = 4
PIECES = 2 * HALF
CROSS = 2
RING = PIECES - CROSS
BACK = 2
HOME = PIECES - BACK


def dot(a, b, dims):
    return lax.dot_general(a, b, (dims, ((), ())), preferred_element_type=F32)


NN = ((1,), (0,))
NT = ((1,), (1,))
TN = ((0,), (0,))


def kernel(
    zn, en,
    ids, prob, tok, cot, wg, wu, wd,
    out_y, out_dx, out_g, out_u, out_d,
    ag, meta_v, wg_v, wu_v, wd_v, rank_v, prob_v, pick_f, prob_f, pick_b, pick_t, hi_t, lo_t,
    send, recv, gate, up, dh, hid, dgu, back, ret, part, rs_s, rs_r, snd_gu, snd_d, rcv_gu, rcv_d,
    l_sem, lw_sem, m_ssem, m_rsem, w_ssem, w_rsem, ag_ssem, ag_rsem, d_ssem, d_rsem, own_sem,
    b_ssem, b_rsem, bown_sem, rs_ssem, rs_rsem, g_ssem, g_rsem,
    ids_v, chance_v, all_rank, all_prob, own_f, own_prob, own_pick, own_hi, own_lo, order,
    x_r, z_s, z_r, back_z_s, back_z_r, back_x, ids_sem, x_ssem, x_rsem, x_own, z_ssem, z_rsem, bz_ssem, bz_rsem,
):
    z = lax.axis_index("grp")
    c = lax.axis_index("exp")
    r = lax.axis_index("rep")
    o = 1 - r
    tn = ag.shape[2]
    w = ag.shape[3]
    rows = RANKS * zn
    slots = en * rows
    ff = gate.shape[1]
    fh = ff // 2
    lanes = 128
    per = lanes // tn
    long = zn // 2

    def hops(p, way):
        return long if (p % 2) == way else zn - 1 - long

    def step(way):
        return 1 if way == 0 else -1

    def there(way):
        return {"grp": lax.rem(z + step(way) + zn, zn)}

    barrier = pltpu.get_barrier_semaphore()
    pl.semaphore_signal(barrier, inc=1, device_id={"rep": o}, device_id_type=MESH)

    def greet_grp(d, carry):
        pl.semaphore_signal(barrier, inc=1, device_id={"grp": lax.rem(z + d, zn)}, device_id_type=MESH)
        return carry

    def greet_exp(d, carry):
        pl.semaphore_signal(barrier, inc=1, device_id={"exp": lax.rem(c + d, en)}, device_id_type=MESH)
        return carry

    lax.fori_loop(1, zn, greet_grp, 0)
    lax.fori_loop(1, en, greet_exp, 0)

    def local(p):
        src = tok if p < HALF else cot
        return pltpu.make_async_copy(
            src.at[:, pl.ds((p % HALF) * w, w)], ag.at[p, z], l_sem.at[p])

    tables_in = [
        pltpu.make_async_copy(ids, ids_v, ids_sem.at[0]),
        pltpu.make_async_copy(prob, chance_v, ids_sem.at[1]),
    ]
    for copy in tables_in:
        copy.start()
    for p in list(range(RING, PIECES)) + list(range(RING)):
        local(p).start()
    wq = HALF // 2
    half_gate = pl.ds(r * wq, wq)
    half_down = pl.ds(pl.multiple_of(r * fh, fh), fh)
    w_local = [
        pltpu.make_async_copy(wg, wg_v.at[half_gate], lw_sem.at[0]),
        pltpu.make_async_copy(wu, wu_v.at[half_gate], lw_sem.at[1]),
    ]
    for q in range(HALF):
        w_local.append(pltpu.make_async_copy(
            wd.at[:, pl.ds(q * w, w)], wd_v.at[q, half_down], lw_sem.at[2 + q]))
    for copy in w_local:
        copy.start()

    lane = lax.broadcasted_iota(jnp.int32, (tn, lanes), 1)
    token = lax.broadcasted_iota(jnp.int32, (tn, lanes), 0)
    spot = ((lane % tn == token) & (lane // tn == lax.rem(z, per))).astype(F32)
    for copy in tables_in:
        copy.wait()
    for i, table in enumerate((ids_v[...].astype(F32), chance_v[...])):
        meta_v[z, 8 * i:8 * i + 8, :] = lax.dot_general(
            table, spot, (NN, ((), ())), precision=lax.Precision.HIGHEST, preferred_element_type=F32)

    row = lax.broadcasted_iota(jnp.int32, (lanes, lanes), 0)
    col = lax.broadcasted_iota(jnp.int32, (lanes, lanes), 1)
    before = ((row < col) & (row // tn == col // tn)).astype(F32).astype(BF16)
    expert = lax.broadcasted_iota(jnp.int32, (en * zn, tn), 0).astype(F32)
    named = jnp.zeros((en * zn, tn), F32)
    weight = jnp.zeros((en * zn, tn), F32)
    for k in range(8):
        hit = ids_v[k:k + 1, :].astype(F32) == expert
        named = named + jnp.where(hit, 1.0, 0.0)
        weight = weight + jnp.where(hit, chance_v[k:k + 1, :], 0.0)
    rank = dot(named.astype(BF16), before[:tn, :tn], NN)
    all_rank[...] = jnp.where(named > 0.0, rank, -1.0)
    all_prob[...] = weight
    for e in range(en):
        seen = all_rank[pl.ds(e, zn, stride=en), :]
        worth = all_prob[pl.ds(e, zn, stride=en), :]
        for k in range(RANKS):
            at = slice((e * RANKS + k) * zn, (e * RANKS + k + 1) * zn)
            own_f[at, :] = jnp.where(seen == float(k), 1.0, 0.0)
            own_prob[at, :] = jnp.where(seen == float(k), worth, 0.0)
    own_pick[...] = own_f[...].astype(BF16)
    near = en * RANKS
    row = lax.broadcasted_iota(jnp.int32, (slots, slots), 0)
    col = lax.broadcasted_iota(jnp.int32, (slots, slots), 1)
    order[...] = ((row // near == col % zn) & (row % near == col // zn)).astype(F32).astype(BF16)
    pl.semaphore_wait(barrier, 1 + (zn - 1) + (en - 1))


    def send_meta(d, carry):
        pltpu.make_async_remote_copy(
            src_ref=meta_v.at[z], dst_ref=meta_v.at[z], send_sem=m_ssem, recv_sem=m_rsem,
            device_id={"grp": lax.rem(z + d, zn)}, device_id_type=MESH).start()
        return carry

    lax.fori_loop(1, zn, send_meta, 0)

    def ring(p, way, s):
        block = lax.rem(z - step(way) * s + zn, zn)
        return pltpu.make_async_remote_copy(
            src_ref=ag.at[p, block], dst_ref=ag.at[p, block],
            send_sem=ag_ssem.at[way], recv_sem=ag_rsem.at[way, p, s],
            device_id=there(way), device_id_type=MESH)

    def ring_recv(p, way, s):
        pltpu.make_async_copy(ag.at[p, 0], ag.at[p, 0], ag_rsem.at[way, p, s]).wait()

    def ring_step(p, s):
        if s == 0:
            local(p).wait()
        for way in (0, 1):
            if s < hops(p, way):
                if s > 0:
                    ring_recv(p, way, s - 1)
                ring(p, way, s).start()

    def ring_sent(sem, way):
        some = ag.at[pl.ds(0, RING // 2), pl.ds(0, zn - 1)]
        pltpu.make_async_copy(some, some, sem.at[way]).wait()

    def weights_out():
        copies = [
            pltpu.make_async_remote_copy(
                src_ref=wg, dst_ref=wg_v.at[half_gate], send_sem=w_ssem.at[0], recv_sem=w_rsem.at[0],
                device_id={"rep": o}, device_id_type=MESH),
            pltpu.make_async_remote_copy(
                src_ref=wu, dst_ref=wu_v.at[half_gate], send_sem=w_ssem.at[1], recv_sem=w_rsem.at[1],
                device_id={"rep": o}, device_id_type=MESH),
        ]
        for q in range(HALF):
            copies.append(pltpu.make_async_remote_copy(
                src_ref=wd.at[:, pl.ds(q * w, w)], dst_ref=wd_v.at[q, half_down],
                send_sem=w_ssem.at[2 + q], recv_sem=w_rsem.at[2 + q],
                device_id={"rep": o}, device_id_type=MESH))
        return copies

    def tables():
        pltpu.make_async_copy(
            meta_v.at[pl.ds(0, zn - 1)], meta_v.at[pl.ds(0, zn - 1)], m_rsem).wait()
        row = lax.broadcasted_iota(jnp.int32, (lanes, lanes), 0)
        col = lax.broadcasted_iota(jnp.int32, (lanes, lanes), 1)
        before = ((row < col) & (row // tn == col // tn)).astype(F32).astype(BF16)
        mine = (lax.broadcasted_iota(jnp.int32, (en, lanes), 0) + en * z).astype(F32)
        sub = lax.broadcasted_iota(jnp.int32, (rows, lanes), 0)
        lane = lax.broadcasted_iota(jnp.int32, (rows, lanes), 1)
        want = (sub // zn).astype(F32)
        for h in range(zn // per):
            both = meta_v[h * per]
            for b in range(1, per):
                both = both + meta_v[h * per + b]
            named = jnp.zeros((en, lanes), F32)
            prob = jnp.zeros((en, lanes), F32)
            for k in range(8):
                hit = both[k:k + 1, :] == mine
                named = named + jnp.where(hit, 1.0, 0.0)
                prob = prob + jnp.where(hit, both[8 + k:9 + k, :], 0.0)
            rank = dot(named.astype(BF16), before, NN)
            rank_v[h] = jnp.where(named > 0.0, rank, -1.0)
            prob_v[h] = prob
            here = (sub % zn) == (h * per + lane // tn)
            for e in range(en):
                hit = (rank_v[h, e:e + 1, :] == want) & here
                at = (slice(e * rows, (e + 1) * rows), slice(h * lanes, (h + 1) * lanes))
                pick_f[at] = jnp.where(hit, 1.0, 0.0)
                prob_f[at] = jnp.where(hit, prob_v[h, e:e + 1, :], 0.0)
        pick_b[...] = pick_f[...].astype(BF16)

    def select(p):
        x = ag[p].reshape(zn * tn, w)
        got = dot(pick_b[...], x, NN)
        if p >= HALF:
            got = got * jnp.sum(prob_f[...], axis=1, keepdims=True)
        send[p] = grouped(got)

    def fan_out(src, i, dst, p, ssem, rsem, osem):
        pltpu.make_async_copy(src.at[i, c], dst.at[p, c], osem.at[p]).start()

        def one(d, carry):
            to = lax.rem(c + d, en)
            pltpu.make_async_remote_copy(
                src_ref=src.at[i, to], dst_ref=dst.at[p, c], send_sem=ssem.at[p], recv_sem=rsem.at[p],
                device_id={"exp": to}, device_id_type=MESH).start()
            return carry

        lax.fori_loop(1, en, one, 0)

    def fan_wait(buf, p, sem):
        pltpu.make_async_copy(
            buf.at[0, pl.ds(0, en - 1)], buf.at[0, pl.ds(0, en - 1)], sem.at[p]).wait()

    def fan_recv(dst, p, rsem, osem):
        fan_wait(dst, p, rsem)
        pltpu.make_async_copy(dst.at[p, 0], dst.at[p, 0], osem.at[p]).wait()

    def grouped(value):
        return value.reshape(slots // 8, 8, w).astype(BF16).reshape(en, rows // 8, 8, w)

    def across(src, dst, i, d, ssem, rsem):
        to = lax.rem(z + d, zn)
        pltpu.make_async_remote_copy(
            src_ref=src.at[i, to], dst_ref=dst.at[i, z], send_sem=ssem.at[i], recv_sem=rsem.at[i],
            device_id={"grp": to}, device_id_type=MESH).start()

    def across_wait(buf, i, sem):
        some = buf.at[i, pl.ds(0, zn - 1)]
        pltpu.make_async_copy(some, some, sem.at[i]).wait()

    def by_group(dst, i, value):
        dst[i] = dot(order[...], value, NN).astype(BF16).reshape(zn, near, w)

    def from_groups(src, own, i):
        src[i, z] = own[i, z]
        return dot(order[...], src[i].reshape(slots, w), TN)

    def select_own(i):
        got = dot(own_pick[...], ag[RING + i, z], NN)
        return got * jnp.sum(own_prob[...], axis=1, keepdims=True)

    def flat(ref, p):
        return ref[p].astype(F32).reshape(slots, w).astype(BF16)

    def take_tokens(p, carry):
        fan_recv(recv, p, d_rsem, own_sem)
        x = flat(recv, p)
        gate[...] += dot(x, wg_v[p], NN)
        up[...] += dot(x, wu_v[p], NN)
        return carry

    chunk = slots // 8

    def forward(i, carry):
        at = pl.ds(pl.multiple_of(i * chunk, chunk), chunk)
        g = gate[at, :]
        hid[at, :] = (g * jax.nn.sigmoid(g) * up[at, :]).astype(BF16)
        return carry


    def give_out(p, carry):
        y = dot(hid[...], wd_v[p], NN)
        back[p] = grouped(y)
        fan_out(back, p, ret, p, b_ssem, b_rsem, bown_sem)
        return carry


    def give_across(i, carry):
        by_group(back_z_s, i, dot(hid[...], wd_v[HALF - BACK + i], NN).astype(BF16))

        def one(d, inner):
            across(back_z_s, back_z_r, i, d, bz_ssem, bz_rsem)
            return inner

        lax.fori_loop(1, zn, one, 0)
        return carry


    def deliver(p):
        for way in (0, 1):
            ring_recv(p, way, hops(p, way) - 1)
        select(p)
        fan_out(send, p, recv, p, d_ssem, d_rsem, own_sem)

    def cross_on(t):
        for i in range(CROSS):
            far = t - long - 1 - i
            if far == -1:
                fan_recv(x_r, i, x_rsem, x_own)
                by_group(z_s, i, flat(x_r, i))
            if 0 < far <= long:
                for d in sorted({far, zn - far}):
                    across(z_s, z_r, i, d, z_ssem, z_rsem)

    for t in range(RING + long):
        p = t - long
        if p == 0:
            tables()
            deliver(p)
        for s in range(long - 1, -1, -1):
            if 0 <= t - s < RING:
                ring_step(t - s, s)
        if t == 0:
            for i in range(CROSS):
                local(RING + i).wait()
                send[RING + i] = grouped(select_own(i))
            for i in range(CROSS):
                fan_out(send, RING + i, x_r, i, x_ssem, x_rsem, x_own)
            for copy in weights_out():
                copy.start()
        if p > 0:
            deliver(p)
        cross_on(t)
        if p == RING - 2:
            gate[...] = jnp.zeros_like(gate)
            up[...] = jnp.zeros_like(up)
            dh[...] = jnp.zeros_like(dh)
            for copy in w_local:
                copy.wait()
            for copy in weights_out():
                copy.wait_recv()
            lax.fori_loop(0, HALF - 1, take_tokens, 0)
    for t in range(RING + long, RING + long + CROSS):
        cross_on(t)
    lax.fori_loop(HALF - 1, HALF, take_tokens, 0)
    lax.fori_loop(0, 8, forward, 0)
    lax.fori_loop(0, BACK, give_across, 0)

    pick_t[...] = pick_f[...].T.astype(BF16)
    prob_t = prob_f[...].T
    hi_t[...] = prob_t.astype(BF16)
    lo_t[...] = (prob_t - prob_t.astype(BF16).astype(F32)).astype(BF16)
    own_t = own_prob[...].T
    own_hi[...] = own_t.astype(BF16)
    own_lo[...] = (own_t - own_t.astype(BF16).astype(F32)).astype(BF16)

    def take_cot(q, carry):
        p = q + HALF
        fan_recv(recv, p, d_rsem, own_sem)
        dh[...] += dot(flat(recv, p), wd_v[q], NT)
        return carry


    def take_across(i, carry):
        across_wait(z_r, i, z_rsem)
        x = from_groups(z_r, z_s, i)
        recv[RING + i] = grouped(x)
        dh[...] += dot(x.astype(BF16), wd_v[HALF - CROSS + i], NT)
        return carry

    lax.fori_loop(0, HALF - CROSS - 1, take_cot, 0)
    lax.fori_loop(0, HALF - BACK, give_out, 0)
    lax.fori_loop(HALF - CROSS - 1, HALF - CROSS, take_cot, 0)
    lax.fori_loop(0, CROSS, take_across, 0)

    def backward(i, carry):
        at = pl.ds(pl.multiple_of(i * chunk, chunk), chunk)
        g = gate[at, :]
        sig = jax.nn.sigmoid(g)
        d = dh[at, :]
        dgu[at, :ff] = (d * up[at, :] * sig * (1.0 + g * (1.0 - sig))).astype(BF16)
        dgu[at, ff:] = (d * (g * sig)).astype(BF16)
        return carry

    lax.fori_loop(0, 8, backward, 0)

    def give_grad(q, carry):
        p = q + HALF
        x = dot(dgu[:, :ff], wg_v[q], NT) + dot(dgu[:, ff:], wu_v[q], NT)
        back[p] = grouped(x)
        fan_out(back, p, ret, p, b_ssem, b_rsem, bown_sem)
        return carry

    lax.fori_loop(0, HALF, give_grad, 0)

    def partial_gu(i, half):
        return dot(flat(recv, half * wq + i), dgu[...], TN).astype(BF16)

    def partial_d(q, half):
        part_hid = hid[:, pl.ds(pl.multiple_of(half * fh, fh), fh)]
        return dot(part_hid, flat(recv, q + HALF), TN).astype(BF16)

    def columns(q):
        return pl.ds(pl.multiple_of(q * w, w), w)

    def other_gu(i, carry):
        snd_gu[i] = partial_gu(i, o)
        return carry

    def other_d(q, carry):
        snd_d[q] = partial_d(q, o)
        return carry

    def own_gu(i, carry):
        both = partial_gu(i, r)
        out_g[i] = both[:, :ff]
        out_u[i] = both[:, ff:]
        return carry

    def own_d(q, carry):
        out_d[:, columns(q)] = partial_d(q, r)
        return carry

    def grads_out():
        return [
            pltpu.make_async_remote_copy(
                src_ref=snd_gu, dst_ref=rcv_gu, send_sem=g_ssem.at[0], recv_sem=g_rsem.at[0],
                device_id={"rep": o}, device_id_type=MESH),
            pltpu.make_async_remote_copy(
                src_ref=snd_d, dst_ref=rcv_d, send_sem=g_ssem.at[1], recv_sem=g_rsem.at[1],
                device_id={"rep": o}, device_id_type=MESH),
        ]

    def combine(p):
        fan_recv(ret, p, b_rsem, bown_sem)
        x = flat(ret, p)
        if p < HALF:
            total = dot(hi_t[...], x, NN) + dot(lo_t[...], x, NN)
        else:
            total = dot(pick_t[...], x, NN)
        part[p] = total.reshape(zn, tn, w)

    rings = list(range(HALF - BACK)) + list(range(HALF, PIECES))

    def rs_send(n, way, s):
        return pltpu.make_async_remote_copy(
            src_ref=rs_s.at[way, n, s], dst_ref=rs_r.at[way, n, s],
            send_sem=rs_ssem.at[way, n], recv_sem=rs_rsem.at[way, n, s],
            device_id=there(way), device_id_type=MESH)

    def rs_step(n, s):
        for way in (0, 1):
            far = hops(n, way)
            if s < far:
                block = lax.rem(z + step(way) * (far - s) + zn, zn)
                value = part[rings[n], block]
                if s > 0:
                    rs_send(n, way, s - 1).wait_recv()
                    value = value + rs_r[way, n, s - 1].astype(F32)
                rs_s[way, n, s] = value.astype(BF16)
                rs_send(n, way, s).start()

    def put(p, value):
        dst = out_y if p < HALF else out_dx
        q = p % HALF
        dst[:, q * w:(q + 1) * w] = value.astype(BF16)

    def rs_final(n):
        value = part[rings[n], z]
        for way in (0, 1):
            far = hops(n, way)
            rs_send(n, way, far - 1).wait_recv()
            value = value + rs_r[way, n, far - 1].astype(F32)
        put(rings[n], value)

    def turn(i):
        across_wait(back_z_r, i, bz_rsem)
        back_x[i] = grouped(from_groups(back_z_r, back_z_s, i))
        fan_out(back_x, i, ret, HALF - BACK + i, b_ssem, b_rsem, bown_sem)

    def arrive(i):
        p = HALF - BACK + i
        fan_recv(ret, p, b_rsem, bown_sem)
        x = flat(ret, p)
        put(p, dot(own_hi[...], x, NN) + dot(own_lo[...], x, NN))

    def finish_gu(i, carry):
        out_g[i] = (out_g[i].astype(F32) + rcv_gu[i, :, :ff].astype(F32)).astype(BF16)
        out_u[i] = (out_u[i].astype(F32) + rcv_gu[i, :, ff:].astype(F32)).astype(BF16)
        return carry

    def finish_d(q, carry):
        out_d[:, columns(q)] = (out_d[:, columns(q)].astype(F32) + rcv_d[q].astype(F32)).astype(BF16)
        return carry

    def fill(t):
        if t < wq:
            other_gu(t, 0)
            if t == wq - 1:
                grads_out()[0].start()
        elif t == wq:
            lax.fori_loop(0, HALF, other_d, 0)
            grads_out()[1].start()
        elif t < 2 * wq + 1:
            own_gu(t - wq - 1, 0)
        elif t == 2 * wq + 1:
            lax.fori_loop(0, HALF, own_d, 0)
        elif t == 2 * wq + 2:
            for copy in grads_out():
                copy.wait_recv()
            lax.fori_loop(0, wq, finish_gu, 0)
            lax.fori_loop(0, HALF, finish_d, 0)
        if t == HOME + 1:
            pltpu.make_async_copy(
                meta_v.at[pl.ds(0, zn - 1)], meta_v.at[pl.ds(0, zn - 1)], m_ssem).wait()
            for copy in weights_out() + grads_out():
                copy.wait_send()
            for way in (0, 1):
                ring_sent(ag_ssem, way)
            for p in range(RING):
                fan_wait(send, p, d_ssem)
            for p in range(PIECES):
                fan_wait(back, p, b_ssem)
            for i in range(CROSS):
                fan_wait(send, i, x_ssem)
                across_wait(z_s, i, z_ssem)
            for i in range(BACK):
                across_wait(back_z_s, i, bz_ssem)

    def when(n, s):
        return n + s + (1 if s > 0 and n < HOME - 1 else 0)

    for t in range(HOME + long + 1):
        for s in range(long - 1, 0, -1):
            for n in range(HOME):
                if when(n, s) == t:
                    rs_step(n, s)
        if t < HOME:
            combine(rings[t])
            rs_step(t, 0)
        for n in range(HOME):
            if when(n, long) == t:
                rs_final(n)
        fill(t)
        if 0 < t <= BACK:
            turn(t - 1)
        if HOME < t <= HOME + BACK:
            arrive(t - HOME - 1)

    for n in range(HOME):
        for way in (0, 1):
            some = ag.at[0, pl.ds(0, hops(n, way))]
            pltpu.make_async_copy(some, some, rs_ssem.at[way, n]).wait()


def write_out(*refs):
    copies = [pltpu.make_async_copy(refs[i], refs[5 + i], refs[10].at[i]) for i in range(5)]
    for copy in copies:
        copy.start()
    for copy in copies:
        copy.wait()


def local(zn, en, tokens, cotangent, expert_ids, gate_probs, gate_weight, up_weight, down_weight):
    tn, d = tokens.shape
    ff = gate_weight.shape[2]
    w = d // HALF
    wq = HALF // 2
    fh = ff // 2
    rows = RANKS * zn
    slots = en * rows
    lanes = 128
    per = lanes // tn
    long = zn // 2
    vm = pltpu.VMEM
    dma = pltpu.SemaphoreType.DMA
    group = (PIECES, en, rows // 8, 8, w)
    scratch = [
        vm((PIECES, zn, tn, w), BF16),
        vm((zn, 16, lanes), F32),
        vm((HALF, w, ff), BF16),
        vm((HALF, w, ff), BF16),
        vm((HALF, ff, w), BF16),
        vm((zn // per, en, lanes), F32),
        vm((zn // per, en, lanes), F32),
        vm((slots, zn * tn), F32),
        vm((slots, zn * tn), F32),
        vm((slots, zn * tn), BF16),
        vm((zn * tn, slots), BF16),
        vm((zn * tn, slots), BF16),
        vm((zn * tn, slots), BF16),
        vm(group, BF16),
        vm(group, BF16),
        vm((slots, ff), F32),
        vm((slots, ff), F32),
        vm((slots, ff), F32),
        vm((slots, ff), BF16),
        vm((slots, 2 * ff), BF16),
        vm(group, BF16),
        vm(group, BF16),
        vm((PIECES, zn, tn, w), F32),
        vm((2, HOME, long, tn, w), BF16),
        vm((2, HOME, long, tn, w), BF16),
        vm((wq, w, 2 * ff), BF16),
        vm((HALF, fh, w), BF16),
        vm((wq, w, 2 * ff), BF16),
        vm((HALF, fh, w), BF16),
        dma((PIECES,)), dma((2 + HALF,)), dma, dma, dma((2 + HALF,)), dma((2 + HALF,)),
        dma((2,)), dma((2, RING, long)), dma((RING,)), dma((RING,)), dma((RING,)),
        dma((PIECES,)), dma((PIECES,)), dma((PIECES,)), dma((2, HOME)), dma((2, HOME, long)),
        dma((2,)), dma((2,)),
        vm((8, tn), jnp.int32),
        vm((8, tn), F32),
        vm((en * zn, tn), F32),
        vm((en * zn, tn), F32),
        vm((slots, tn), F32),
        vm((slots, tn), F32),
        vm((slots, tn), BF16),
        vm((tn, slots), BF16),
        vm((tn, slots), BF16),
        vm((slots, slots), BF16),
        vm((CROSS,) + group[1:], BF16),
        vm((CROSS, zn, en * RANKS, w), BF16),
        vm((CROSS, zn, en * RANKS, w), BF16),
        vm((BACK, zn, en * RANKS, w), BF16),
        vm((BACK, zn, en * RANKS, w), BF16),
        vm((BACK,) + group[1:], BF16),
        dma((2,)), dma((CROSS,)), dma((CROSS,)), dma((CROSS,)), dma((CROSS,)), dma((CROSS,)),
        dma((BACK,)), dma((BACK,)),
    ]
    hbm = pl.BlockSpec(memory_space=pl.ANY)
    y, dx, g, u, dd = pl.pallas_call(
        functools.partial(kernel, zn, en),
        out_shape=(
            pltpu.VMEM((tn, d), BF16),
            pltpu.VMEM((tn, d), BF16),
            pltpu.VMEM((wq, w, ff), BF16),
            pltpu.VMEM((wq, w, ff), BF16),
            pltpu.VMEM((fh, d), BF16),
        ),
        in_specs=[hbm] * 7,
        out_specs=(pl.BlockSpec(memory_space=pltpu.VMEM),) * 5,
        scratch_shapes=scratch,
        name="moe",
        compiler_params=pltpu.CompilerParams(
            collective_id=0, has_side_effects=True, vmem_limit_bytes=58000000),
    )(
        expert_ids.T, gate_probs.T, tokens, cotangent,
        gate_weight.reshape(wq, w, ff), up_weight.reshape(wq, w, ff), down_weight.reshape(fh, d),
    )
    made = [pltpu.with_memory_space_constraint(a, pltpu.VMEM) for a in (y, dx, g, u, dd)]
    y, dx, g, u, dd = pl.pallas_call(
        write_out,
        out_shape=tuple(jax.ShapeDtypeStruct(a.shape, BF16) for a in made),
        in_specs=[pl.BlockSpec(memory_space=pltpu.VMEM)] * 5,
        out_specs=(hbm,) * 5,
        scratch_shapes=[dma((5,))],
        name="write_out",
        compiler_params=pltpu.CompilerParams(vmem_limit_bytes=1 << 20),
    )(*made)
    return y, dx, g.reshape(1, wq * w, ff), u.reshape(1, wq * w, ff), dd.reshape(1, fh, d)


def solution(mesh):
    tokens = P(("grp", "exp", "rep"), None)
    weight = P(("grp", "exp"), "rep", None)
    return jax.shard_map(
        functools.partial(local, mesh.shape["grp"], mesh.shape["exp"]),
        mesh=mesh,
        in_specs=(tokens,) * 4 + (weight,) * 3,
        out_specs=(tokens,) * 2 + (weight,) * 3,
        check_vma=False,
    )
```

```python
import functools

import jax
import jax.numpy as jnp
from jax import lax
from jax.experimental import pallas as pl
from jax.experimental.pallas import tpu as pltpu
from jax.sharding import PartitionSpec as P

MESH = pl.DeviceIdType.MESH
F32 = jnp.float32
BF16 = jnp.bfloat16
RANKS = 3
HALF = 4
PIECES = 2 * HALF
CROSS = 2
RING = PIECES - CROSS
BACK = 2
HOME = PIECES - BACK


def dot(a, b, dims):
    return lax.dot_general(a, b, (dims, ((), ())), preferred_element_type=F32)


NN = ((1,), (0,))
NT = ((1,), (1,))
TN = ((0,), (0,))


def kernel(
    zn, en,
    ids, prob, tok, cot, wg, wu, wd,
    out_y, out_dx, out_g, out_u, out_d,
    ag, meta_v, wg_v, wu_v, wd_v, rank_v, prob_v, pick_f, prob_f, pick_b, pick_t, hi_t, lo_t,
    send, recv, gate, up, dh, hid, dgu, back, ret, part, rs_s, rs_r, snd_gu, snd_d, rcv_gu, rcv_d,
    l_sem, lw_sem, m_ssem, m_rsem, w_ssem, w_rsem, ag_ssem, ag_rsem, d_ssem, d_rsem, own_sem,
    b_ssem, b_rsem, bown_sem, rs_ssem, rs_rsem, g_ssem, g_rsem,
    ids_v, chance_v, all_rank, all_prob, own_f, own_prob, own_pick, own_hi, own_lo, order,
    x_r, z_s, z_r, back_z_s, back_z_r, back_x, ids_sem, x_ssem, x_rsem, x_own, z_ssem, z_rsem, bz_ssem, bz_rsem,
):
    z = lax.axis_index("grp")
    c = lax.axis_index("exp")
    r = lax.axis_index("rep")
    o = 1 - r
    tn = ag.shape[2]
    w = ag.shape[3]
    rows = RANKS * zn
    slots = en * rows
    ff = gate.shape[1]
    fh = ff // 2
    lanes = 128
    per = lanes // tn
    long = zn // 2
    near = en * RANKS

    def hops(p, way):
        return long if (p % 2) == way else zn - 1 - long

    def step(way):
        return 1 if way == 0 else -1

    def there(way):
        return {"grp": lax.rem(z + step(way) + zn, zn)}

    barrier = pltpu.get_barrier_semaphore()
    pl.semaphore_signal(barrier, inc=1, device_id={"rep": o}, device_id_type=MESH)

    def greet_grp(d, carry):
        pl.semaphore_signal(barrier, inc=1, device_id={"grp": lax.rem(z + d, zn)}, device_id_type=MESH)
        return carry

    def greet_exp(d, carry):
        pl.semaphore_signal(barrier, inc=1, device_id={"exp": lax.rem(c + d, en)}, device_id_type=MESH)
        return carry

    lax.fori_loop(1, zn, greet_grp, 0)
    lax.fori_loop(1, en, greet_exp, 0)

    def local(p):
        src = tok if p < HALF else cot
        return pltpu.make_async_copy(
            src.at[:, pl.ds((p % HALF) * w, w)], ag.at[p, z], l_sem.at[p])

    tables_in = [
        pltpu.make_async_copy(ids, ids_v, ids_sem.at[0]),
        pltpu.make_async_copy(prob, chance_v, ids_sem.at[1]),
    ]
    for copy in tables_in:
        copy.start()
    for p in [0] + list(range(RING, PIECES)) + list(range(1, RING)):
        local(p).start()
    wq = HALF // 2
    half_gate = pl.ds(r * wq, wq)
    half_down = pl.ds(pl.multiple_of(r * fh, fh), fh)
    w_local = [
        pltpu.make_async_copy(wg, wg_v.at[half_gate], lw_sem.at[0]),
        pltpu.make_async_copy(wu, wu_v.at[half_gate], lw_sem.at[1]),
    ]
    for q in range(HALF):
        w_local.append(pltpu.make_async_copy(
            wd.at[:, pl.ds(q * w, w)], wd_v.at[q, half_down], lw_sem.at[2 + q]))
    for copy in w_local:
        copy.start()

    pl.semaphore_wait(barrier, 1 + (zn - 1) + (en - 1))

    def own_tables():
        lane = lax.broadcasted_iota(jnp.int32, (tn, lanes), 1)
        token = lax.broadcasted_iota(jnp.int32, (tn, lanes), 0)
        spot = ((lane % tn == token) & (lane // tn == lax.rem(z, per))).astype(F32)
        for copy in tables_in:
            copy.wait()
        for i, table in enumerate((ids_v[...].astype(F32), chance_v[...])):
            meta_v[z, 8 * i:8 * i + 8, :] = lax.dot_general(
                table, spot, (NN, ((), ())), precision=lax.Precision.HIGHEST, preferred_element_type=F32)

        row = lax.broadcasted_iota(jnp.int32, (lanes, lanes), 0)
        col = lax.broadcasted_iota(jnp.int32, (lanes, lanes), 1)
        before = ((row < col) & (row // tn == col // tn)).astype(F32).astype(BF16)
        expert = lax.broadcasted_iota(jnp.int32, (en * zn, tn), 0).astype(F32)
        named = jnp.zeros((en * zn, tn), F32)
        weight = jnp.zeros((en * zn, tn), F32)
        for k in range(8):
            hit = ids_v[k:k + 1, :].astype(F32) == expert
            named = named + jnp.where(hit, 1.0, 0.0)
            weight = weight + jnp.where(hit, chance_v[k:k + 1, :], 0.0)
        rank = dot(named.astype(BF16), before[:tn, :tn], NN)
        all_rank[...] = jnp.where(named > 0.0, rank, -1.0)
        all_prob[...] = weight
        for e in range(en):
            seen = all_rank[pl.ds(e, zn, stride=en), :]
            worth = all_prob[pl.ds(e, zn, stride=en), :]
            for k in range(RANKS):
                at = slice((e * RANKS + k) * zn, (e * RANKS + k + 1) * zn)
                own_f[at, :] = jnp.where(seen == float(k), 1.0, 0.0)
                own_prob[at, :] = jnp.where(seen == float(k), worth, 0.0)
        own_pick[...] = own_f[...].astype(BF16)
        row = lax.broadcasted_iota(jnp.int32, (slots, slots), 0)
        col = lax.broadcasted_iota(jnp.int32, (slots, slots), 1)
        order[...] = ((row // near == col % zn) & (row % near == col // zn)).astype(F32).astype(BF16)


        def send_meta(d, carry):
            pltpu.make_async_remote_copy(
                src_ref=meta_v.at[z], dst_ref=meta_v.at[z], send_sem=m_ssem, recv_sem=m_rsem,
                device_id={"grp": lax.rem(z + d, zn)}, device_id_type=MESH).start()
            return carry

        lax.fori_loop(1, zn, send_meta, 0)

    def ring(p, way, s):
        block = lax.rem(z - step(way) * s + zn, zn)
        return pltpu.make_async_remote_copy(
            src_ref=ag.at[p, block], dst_ref=ag.at[p, block],
            send_sem=ag_ssem.at[way], recv_sem=ag_rsem.at[way, p, s],
            device_id=there(way), device_id_type=MESH)

    def ring_recv(p, way, s):
        pltpu.make_async_copy(ag.at[p, 0], ag.at[p, 0], ag_rsem.at[way, p, s]).wait()

    def ring_step(p, s):
        if s == 0:
            local(p).wait()
        for way in (0, 1):
            if s < hops(p, way):
                if s > 0:
                    ring_recv(p, way, s - 1)
                ring(p, way, s).start()

    def ring_sent(sem, way):
        some = ag.at[pl.ds(0, RING // 2), pl.ds(0, zn - 1)]
        pltpu.make_async_copy(some, some, sem.at[way]).wait()

    def weights_out():
        copies = [
            pltpu.make_async_remote_copy(
                src_ref=wg, dst_ref=wg_v.at[half_gate], send_sem=w_ssem.at[0], recv_sem=w_rsem.at[0],
                device_id={"rep": o}, device_id_type=MESH),
            pltpu.make_async_remote_copy(
                src_ref=wu, dst_ref=wu_v.at[half_gate], send_sem=w_ssem.at[1], recv_sem=w_rsem.at[1],
                device_id={"rep": o}, device_id_type=MESH),
        ]
        for q in range(HALF):
            copies.append(pltpu.make_async_remote_copy(
                src_ref=wd.at[:, pl.ds(q * w, w)], dst_ref=wd_v.at[q, half_down],
                send_sem=w_ssem.at[2 + q], recv_sem=w_rsem.at[2 + q],
                device_id={"rep": o}, device_id_type=MESH))
        return copies

    def tables():
        pltpu.make_async_copy(
            meta_v.at[pl.ds(0, zn - 1)], meta_v.at[pl.ds(0, zn - 1)], m_rsem).wait()
        row = lax.broadcasted_iota(jnp.int32, (lanes, lanes), 0)
        col = lax.broadcasted_iota(jnp.int32, (lanes, lanes), 1)
        before = ((row < col) & (row // tn == col // tn)).astype(F32).astype(BF16)
        mine = (lax.broadcasted_iota(jnp.int32, (en, lanes), 0) + en * z).astype(F32)
        sub = lax.broadcasted_iota(jnp.int32, (rows, lanes), 0)
        lane = lax.broadcasted_iota(jnp.int32, (rows, lanes), 1)
        want = (sub // zn).astype(F32)
        for h in range(zn // per):
            both = meta_v[h * per]
            for b in range(1, per):
                both = both + meta_v[h * per + b]
            named = jnp.zeros((en, lanes), F32)
            prob = jnp.zeros((en, lanes), F32)
            for k in range(8):
                hit = both[k:k + 1, :] == mine
                named = named + jnp.where(hit, 1.0, 0.0)
                prob = prob + jnp.where(hit, both[8 + k:9 + k, :], 0.0)
            rank = dot(named.astype(BF16), before, NN)
            rank_v[h] = jnp.where(named > 0.0, rank, -1.0)
            prob_v[h] = prob
            here = (sub % zn) == (h * per + lane // tn)
            for e in range(en):
                hit = (rank_v[h, e:e + 1, :] == want) & here
                at = (slice(e * rows, (e + 1) * rows), slice(h * lanes, (h + 1) * lanes))
                pick_f[at] = jnp.where(hit, 1.0, 0.0)
                prob_f[at] = jnp.where(hit, prob_v[h, e:e + 1, :], 0.0)
        pick_b[...] = pick_f[...].astype(BF16)

    def select(p):
        x = ag[p].reshape(zn * tn, w)
        got = dot(pick_b[...], x, NN)
        if p >= HALF:
            got = got * jnp.sum(prob_f[...], axis=1, keepdims=True)
        send[p] = grouped(got)

    def fan_out(src, i, dst, p, ssem, rsem, osem):
        pltpu.make_async_copy(src.at[i, c], dst.at[p, c], osem.at[p]).start()

        def one(d, carry):
            to = lax.rem(c + d, en)
            pltpu.make_async_remote_copy(
                src_ref=src.at[i, to], dst_ref=dst.at[p, c], send_sem=ssem.at[p], recv_sem=rsem.at[p],
                device_id={"exp": to}, device_id_type=MESH).start()
            return carry

        lax.fori_loop(1, en, one, 0)

    def fan_wait(buf, p, sem):
        pltpu.make_async_copy(
            buf.at[0, pl.ds(0, en - 1)], buf.at[0, pl.ds(0, en - 1)], sem.at[p]).wait()

    def fan_recv(dst, p, rsem, osem):
        fan_wait(dst, p, rsem)
        pltpu.make_async_copy(dst.at[p, 0], dst.at[p, 0], osem.at[p]).wait()

    def grouped(value):
        return value.reshape(slots // 8, 8, w).astype(BF16).reshape(en, rows // 8, 8, w)

    def across(src, dst, i, d, ssem, rsem):
        to = lax.rem(z + d, zn)
        pltpu.make_async_remote_copy(
            src_ref=src.at[i, to], dst_ref=dst.at[i, z], send_sem=ssem.at[i], recv_sem=rsem.at[i],
            device_id={"grp": to}, device_id_type=MESH).start()

    def across_wait(buf, i, sem):
        some = buf.at[i, pl.ds(0, zn - 1)]
        pltpu.make_async_copy(some, some, sem.at[i]).wait()

    def by_group(dst, i, value):
        dst[i] = dot(order[...], value, NN).astype(BF16).reshape(zn, near, w)

    def from_groups(src, own, i):
        src[i, z] = own[i, z]
        return dot(order[...], src[i].reshape(slots, w), TN)

    def select_own(i):
        got = dot(own_pick[...], ag[RING + i, z], NN)
        return got * jnp.sum(own_prob[...], axis=1, keepdims=True)

    def flat(ref, p):
        return ref[p].astype(F32).reshape(slots, w).astype(BF16)

    def take_tokens(p, carry):
        fan_recv(recv, p, d_rsem, own_sem)
        x = flat(recv, p)
        gate[...] += dot(x, wg_v[p], NN)
        up[...] += dot(x, wu_v[p], NN)
        return carry

    chunk = slots // 8

    def forward(i, carry):
        at = pl.ds(pl.multiple_of(i * chunk, chunk), chunk)
        g = gate[at, :]
        hid[at, :] = (g * jax.nn.sigmoid(g) * up[at, :]).astype(BF16)
        return carry


    def give_out(p, carry):
        y = dot(hid[...], wd_v[p], NN)
        back[p] = grouped(y)
        fan_out(back, p, ret, p, b_ssem, b_rsem, bown_sem)
        return carry


    def give_across(i, carry):
        by_group(back_z_s, i, dot(hid[...], wd_v[HALF - BACK + i], NN).astype(BF16))

        def one(d, inner):
            across(back_z_s, back_z_r, i, d, bz_ssem, bz_rsem)
            return inner

        lax.fori_loop(1, zn, one, 0)
        return carry


    def deliver(p):
        for way in (0, 1):
            ring_recv(p, way, hops(p, way) - 1)
        select(p)
        fan_out(send, p, recv, p, d_ssem, d_rsem, own_sem)

    def cross_on(t):
        for i in range(CROSS):
            far = t - long - 1 - i
            if far == -1:
                fan_recv(x_r, i, x_rsem, x_own)
                by_group(z_s, i, flat(x_r, i))
            if 0 < far <= long:
                for d in sorted({far, zn - far}):
                    across(z_s, z_r, i, d, z_ssem, z_rsem)

    for t in range(RING + long):
        p = t - long
        if p == 0:
            tables()
            deliver(p)
        for s in range(long - 1, -1, -1):
            if 0 <= t - s < RING:
                ring_step(t - s, s)
        if t == 0:
            own_tables()
            for i in range(CROSS):
                local(RING + i).wait()
                send[RING + i] = grouped(select_own(i))
            for i in range(CROSS):
                fan_out(send, RING + i, x_r, i, x_ssem, x_rsem, x_own)
            for copy in weights_out():
                copy.start()
        if p > 0:
            deliver(p)
        cross_on(t)
        if p == RING - 2:
            gate[...] = jnp.zeros_like(gate)
            up[...] = jnp.zeros_like(up)
            dh[...] = jnp.zeros_like(dh)
            for copy in w_local:
                copy.wait()
            for copy in weights_out():
                copy.wait_recv()
            lax.fori_loop(0, HALF - 1, take_tokens, 0)
    for t in range(RING + long, RING + long + CROSS):
        cross_on(t)
    lax.fori_loop(HALF - 1, HALF, take_tokens, 0)
    lax.fori_loop(0, 8, forward, 0)
    lax.fori_loop(0, BACK, give_across, 0)

    pick_t[...] = pick_f[...].T.astype(BF16)
    prob_t = prob_f[...].T
    hi_t[...] = prob_t.astype(BF16)
    lo_t[...] = (prob_t - prob_t.astype(BF16).astype(F32)).astype(BF16)
    own_t = own_prob[...].T
    own_hi[...] = own_t.astype(BF16)
    own_lo[...] = (own_t - own_t.astype(BF16).astype(F32)).astype(BF16)

    def take_cot(q, carry):
        p = q + HALF
        fan_recv(recv, p, d_rsem, own_sem)
        dh[...] += dot(flat(recv, p), wd_v[q], NT)
        return carry


    def take_across(i, carry):
        across_wait(z_r, i, z_rsem)
        x = from_groups(z_r, z_s, i)
        recv[RING + i] = grouped(x)
        dh[...] += dot(x.astype(BF16), wd_v[HALF - CROSS + i], NT)
        return carry

    lax.fori_loop(0, HALF - CROSS - 1, take_cot, 0)
    lax.fori_loop(0, HALF - BACK, give_out, 0)
    lax.fori_loop(HALF - CROSS - 1, HALF - CROSS, take_cot, 0)
    lax.fori_loop(0, CROSS, take_across, 0)

    def backward(i, carry):
        at = pl.ds(pl.multiple_of(i * chunk, chunk), chunk)
        g = gate[at, :]
        sig = jax.nn.sigmoid(g)
        d = dh[at, :]
        dgu[at, :ff] = (d * up[at, :] * sig * (1.0 + g * (1.0 - sig))).astype(BF16)
        dgu[at, ff:] = (d * (g * sig)).astype(BF16)
        return carry

    lax.fori_loop(0, 8, backward, 0)

    def give_grad(q, carry):
        p = q + HALF
        x = dot(dgu[:, :ff], wg_v[q], NT) + dot(dgu[:, ff:], wu_v[q], NT)
        back[p] = grouped(x)
        fan_out(back, p, ret, p, b_ssem, b_rsem, bown_sem)
        return carry

    lax.fori_loop(0, HALF, give_grad, 0)

    def partial_gu(i, half):
        return dot(flat(recv, half * wq + i), dgu[...], TN).astype(BF16)

    def partial_d(q, half):
        part_hid = hid[:, pl.ds(pl.multiple_of(half * fh, fh), fh)]
        return dot(part_hid, flat(recv, q + HALF), TN).astype(BF16)

    def columns(q):
        return pl.ds(pl.multiple_of(q * w, w), w)

    def other_gu(i, carry):
        snd_gu[i] = partial_gu(i, o)
        return carry

    def other_d(q, carry):
        snd_d[q] = partial_d(q, o)
        return carry

    def own_gu(i, carry):
        both = partial_gu(i, r)
        out_g[i] = both[:, :ff]
        out_u[i] = both[:, ff:]
        return carry

    def own_d(q, carry):
        out_d[:, columns(q)] = partial_d(q, r)
        return carry

    def grads_out():
        return [
            pltpu.make_async_remote_copy(
                src_ref=snd_gu, dst_ref=rcv_gu, send_sem=g_ssem.at[0], recv_sem=g_rsem.at[0],
                device_id={"rep": o}, device_id_type=MESH),
            pltpu.make_async_remote_copy(
                src_ref=snd_d, dst_ref=rcv_d, send_sem=g_ssem.at[1], recv_sem=g_rsem.at[1],
                device_id={"rep": o}, device_id_type=MESH),
        ]

    def combine(p):
        fan_recv(ret, p, b_rsem, bown_sem)
        x = flat(ret, p)
        if p < HALF:
            total = dot(hi_t[...], x, NN) + dot(lo_t[...], x, NN)
        else:
            total = dot(pick_t[...], x, NN)
        part[p] = total.reshape(zn, tn, w)

    rings = list(range(HALF - BACK)) + list(range(HALF, PIECES))

    def rs_send(n, way, s):
        return pltpu.make_async_remote_copy(
            src_ref=rs_s.at[way, n, s], dst_ref=rs_r.at[way, n, s],
            send_sem=rs_ssem.at[way, n], recv_sem=rs_rsem.at[way, n, s],
            device_id=there(way), device_id_type=MESH)

    def rs_step(n, s):
        for way in (0, 1):
            far = hops(n, way)
            if s < far:
                block = lax.rem(z + step(way) * (far - s) + zn, zn)
                value = part[rings[n], block]
                if s > 0:
                    rs_send(n, way, s - 1).wait_recv()
                    value = value + rs_r[way, n, s - 1].astype(F32)
                rs_s[way, n, s] = value.astype(BF16)
                rs_send(n, way, s).start()

    def put(p, value):
        dst = out_y if p < HALF else out_dx
        q = p % HALF
        dst[:, q * w:(q + 1) * w] = value.astype(BF16)

    def rs_final(n):
        value = part[rings[n], z]
        for way in (0, 1):
            far = hops(n, way)
            rs_send(n, way, far - 1).wait_recv()
            value = value + rs_r[way, n, far - 1].astype(F32)
        put(rings[n], value)

    def turn(i):
        across_wait(back_z_r, i, bz_rsem)
        back_x[i] = grouped(from_groups(back_z_r, back_z_s, i))
        fan_out(back_x, i, ret, HALF - BACK + i, b_ssem, b_rsem, bown_sem)

    def arrive(i):
        p = HALF - BACK + i
        fan_recv(ret, p, b_rsem, bown_sem)
        x = flat(ret, p)
        put(p, dot(own_hi[...], x, NN) + dot(own_lo[...], x, NN))

    def finish_gu(i, carry):
        out_g[i] = (out_g[i].astype(F32) + rcv_gu[i, :, :ff].astype(F32)).astype(BF16)
        out_u[i] = (out_u[i].astype(F32) + rcv_gu[i, :, ff:].astype(F32)).astype(BF16)
        return carry

    def finish_d(q, carry):
        out_d[:, columns(q)] = (out_d[:, columns(q)].astype(F32) + rcv_d[q].astype(F32)).astype(BF16)
        return carry

    def fill(t):
        if t < wq:
            other_gu(t, 0)
            if t == wq - 1:
                grads_out()[0].start()
        elif t == wq:
            lax.fori_loop(0, HALF, other_d, 0)
            grads_out()[1].start()
        elif t < 2 * wq + 1:
            own_gu(t - wq - 1, 0)
        elif t == 2 * wq + 1:
            lax.fori_loop(0, HALF, own_d, 0)
        elif t == 2 * wq + 2:
            for copy in grads_out():
                copy.wait_recv()
            lax.fori_loop(0, wq, finish_gu, 0)
            lax.fori_loop(0, HALF, finish_d, 0)
        if t == HOME + 1:
            pltpu.make_async_copy(
                meta_v.at[pl.ds(0, zn - 1)], meta_v.at[pl.ds(0, zn - 1)], m_ssem).wait()
            for copy in weights_out() + grads_out():
                copy.wait_send()
            for way in (0, 1):
                ring_sent(ag_ssem, way)
            for p in range(RING):
                fan_wait(send, p, d_ssem)
            for p in range(PIECES):
                fan_wait(back, p, b_ssem)
            for i in range(CROSS):
                fan_wait(send, i, x_ssem)
                across_wait(z_s, i, z_ssem)
            for i in range(BACK):
                across_wait(back_z_s, i, bz_ssem)

    def when(n, s):
        return n + s + (1 if s > 0 and n < HOME - 2 else 0)

    for t in range(HOME + long + 1):
        for s in range(long - 1, 0, -1):
            for n in range(HOME):
                if when(n, s) == t:
                    rs_step(n, s)
        if t < HOME:
            combine(rings[t])
            rs_step(t, 0)
        for n in range(HOME):
            if when(n, long) == t:
                rs_final(n)
        fill(t)
        if 0 < t <= BACK:
            turn(t - 1)
        if HOME < t <= HOME + BACK:
            arrive(t - HOME - 1)

    for n in range(HOME):
        for way in (0, 1):
            some = ag.at[0, pl.ds(0, hops(n, way))]
            pltpu.make_async_copy(some, some, rs_ssem.at[way, n]).wait()


def write_out(*refs):
    copies = [pltpu.make_async_copy(refs[i], refs[5 + i], refs[10].at[i]) for i in range(5)]
    for copy in copies:
        copy.start()
    for copy in copies:
        copy.wait()


def local(zn, en, tokens, cotangent, expert_ids, gate_probs, gate_weight, up_weight, down_weight):
    tn, d = tokens.shape
    ff = gate_weight.shape[2]
    w = d // HALF
    wq = HALF // 2
    fh = ff // 2
    rows = RANKS * zn
    slots = en * rows
    lanes = 128
    per = lanes // tn
    long = zn // 2
    vm = pltpu.VMEM
    dma = pltpu.SemaphoreType.DMA
    group = (PIECES, en, rows // 8, 8, w)
    scratch = [
        vm((PIECES, zn, tn, w), BF16),
        vm((zn, 16, lanes), F32),
        vm((HALF, w, ff), BF16),
        vm((HALF, w, ff), BF16),
        vm((HALF, ff, w), BF16),
        vm((zn // per, en, lanes), F32),
        vm((zn // per, en, lanes), F32),
        vm((slots, zn * tn), F32),
        vm((slots, zn * tn), F32),
        vm((slots, zn * tn), BF16),
        vm((zn * tn, slots), BF16),
        vm((zn * tn, slots), BF16),
        vm((zn * tn, slots), BF16),
        vm(group, BF16),
        vm(group, BF16),
        vm((slots, ff), F32),
        vm((slots, ff), F32),
        vm((slots, ff), F32),
        vm((slots, ff), BF16),
        vm((slots, 2 * ff), BF16),
        vm(group, BF16),
        vm(group, BF16),
        vm((PIECES, zn, tn, w), F32),
        vm((2, HOME, long, tn, w), BF16),
        vm((2, HOME, long, tn, w), BF16),
        vm((wq, w, 2 * ff), BF16),
        vm((HALF, fh, w), BF16),
        vm((wq, w, 2 * ff), BF16),
        vm((HALF, fh, w), BF16),
        dma((PIECES,)), dma((2 + HALF,)), dma, dma, dma((2 + HALF,)), dma((2 + HALF,)),
        dma((2,)), dma((2, RING, long)), dma((RING,)), dma((RING,)), dma((RING,)),
        dma((PIECES,)), dma((PIECES,)), dma((PIECES,)), dma((2, HOME)), dma((2, HOME, long)),
        dma((2,)), dma((2,)),
        vm((8, tn), jnp.int32),
        vm((8, tn), F32),
        vm((en * zn, tn), F32),
        vm((en * zn, tn), F32),
        vm((slots, tn), F32),
        vm((slots, tn), F32),
        vm((slots, tn), BF16),
        vm((tn, slots), BF16),
        vm((tn, slots), BF16),
        vm((slots, slots), BF16),
        vm((CROSS,) + group[1:], BF16),
        vm((CROSS, zn, en * RANKS, w), BF16),
        vm((CROSS, zn, en * RANKS, w), BF16),
        vm((BACK, zn, en * RANKS, w), BF16),
        vm((BACK, zn, en * RANKS, w), BF16),
        vm((BACK,) + group[1:], BF16),
        dma((2,)), dma((CROSS,)), dma((CROSS,)), dma((CROSS,)), dma((CROSS,)), dma((CROSS,)),
        dma((BACK,)), dma((BACK,)),
    ]
    hbm = pl.BlockSpec(memory_space=pl.ANY)
    y, dx, g, u, dd = pl.pallas_call(
        functools.partial(kernel, zn, en),
        out_shape=(
            pltpu.VMEM((tn, d), BF16),
            pltpu.VMEM((tn, d), BF16),
            pltpu.VMEM((wq, w, ff), BF16),
            pltpu.VMEM((wq, w, ff), BF16),
            pltpu.VMEM((fh, d), BF16),
        ),
        in_specs=[hbm] * 7,
        out_specs=(pl.BlockSpec(memory_space=pltpu.VMEM),) * 5,
        scratch_shapes=scratch,
        name="moe",
        compiler_params=pltpu.CompilerParams(
            collective_id=0, has_side_effects=True, vmem_limit_bytes=58000000),
    )(
        expert_ids.T, gate_probs.T, tokens, cotangent,
        gate_weight.reshape(wq, w, ff), up_weight.reshape(wq, w, ff), down_weight.reshape(fh, d),
    )
    made = [pltpu.with_memory_space_constraint(a, pltpu.VMEM) for a in (y, dx, g, u, dd)]
    y, dx, g, u, dd = pl.pallas_call(
        write_out,
        out_shape=tuple(jax.ShapeDtypeStruct(a.shape, BF16) for a in made),
        in_specs=[pl.BlockSpec(memory_space=pltpu.VMEM)] * 5,
        out_specs=(hbm,) * 5,
        scratch_shapes=[dma((5,))],
        name="write_out",
        compiler_params=pltpu.CompilerParams(vmem_limit_bytes=1 << 20),
    )(*made)
    return y, dx, g.reshape(1, wq * w, ff), u.reshape(1, wq * w, ff), dd.reshape(1, fh, d)


def solution(mesh):
    tokens = P(("grp", "exp", "rep"), None)
    weight = P(("grp", "exp"), "rep", None)
    return jax.shard_map(
        functools.partial(local, mesh.shape["grp"], mesh.shape["exp"]),
        mesh=mesh,
        in_specs=(tokens,) * 4 + (weight,) * 3,
        out_specs=(tokens,) * 2 + (weight,) * 3,
        check_vma=False,
    )
```
